512 devices in a mesh: dp: 4 (over y), grp: 4 (over x), loc: 32 (over z, core).
Axes of the slice: x: 4, y: 4, z: 16, core: 2. Of those that a mesh axis runs over, the one named last changes fastest.
Arguments:
- tokens: bfloat16 [16384, 2048], P(('grp', 'loc'), 'dp'), may hold values from -6 to 6
- grad_out: bfloat16 [16384, 2048], P(('grp', 'loc'), 'dp'), may hold values from -6 to 6
- expert_ids: int32 [16384, 4], P(('grp', 'loc')), may hold values from 0 to 127, all different within a row; in each aligned block of 128 rows (0 to 127, 128 to 255, ...) at most 8 rows name the same one
- gate_scale: float32 [16384, 4], P(('grp', 'loc')), may hold values from 0.1 to 1
- gate_weight: bfloat16 [128, 768, 2048], P(('grp', 'loc'), 'dp'), may hold values from -0.125 to 0.125
- up_weight: bfloat16 [128, 768, 2048], P(('grp', 'loc'), 'dp'), may hold values from -0.125 to 0.125
- down_weight: bfloat16 [128, 768, 2048], P(('grp', 'loc'), None, 'dp'), may hold values from -0.21875 to 0.21875
Outputs:
- layer_out: bfloat16 [16384, 2048], P(('grp', 'loc'), 'dp')
- gate_gradient: bfloat16 [128, 768, 2048], P(('grp', 'loc'), 'dp')
- up_gradient: bfloat16 [128, 768, 2048], P(('grp', 'loc'), 'dp')
- down_gradient: bfloat16 [128, 768, 2048], P(('grp', 'loc'), None, 'dp')
The draws below stay inside these ranges and needn't reach their ends.
Inputs may be any that keep to these rules, and one draw needn't show every extreme that they name: `expert_ids`: each token names 4 different experts. Within one index of grp and loc (aligned blocks of 128 token rows) no expert is named by more than 8 rows, a bound that some block reaches.
All inputs are finite; a program needn't handle non-finite values.
Results may differ from the reference program's by a relative error of at most 0.0058.
Values may be sent and summed in bfloat16 or wider, within the bound.
A program may use at most 64 MiB of HBM per device.

```python
import math
import jax
import jax.numpy as jnp
import numpy as np
from jax import lax

D = 2048
F = 768
TOP = 4
TOK_DEV = 128
EXPERTS = 128
CAP = 8
TOKENS = 16384


def steps_of(rng, shape, cuts, least, largest):
    gain = 1.0
    for position, parts in cuts:
        draws = jax.random.uniform(jax.random.fold_in(jax.random.fold_in(rng, 6), position), (parts,), jnp.float32, least / len(cuts), largest / len(cuts))
        gain = gain * jnp.repeat(jnp.exp(draws), shape[position] // parts).reshape((-1,) + (1,) * (len(shape) - 1 - position))
    return gain


def assign_block(stream_key, own, number, rows, amount, top, limit, skew):
    ranking = jax.random.permutation(stream_key, amount)
    heavy_load, common = load_shares(amount, rows * top, limit, skew, True), load_shares(amount, rows * top, limit, skew, False)
    places = jnp.arange(amount)

    def named(sizes, offset_by):
        used = int((sizes > 0).sum())
        fixed = max(1, used // 4)
        shifted = fixed + (places - fixed + offset_by * (used - fixed)) % max(1, amount - fixed)
        return jnp.zeros((amount,), jnp.int32).at[ranking[jnp.where(places < fixed, places, shifted)]].set(jnp.asarray(sizes, jnp.int32))

    sizes = jnp.where(number % 4 == 0, named(heavy_load, number // 4), named(common, number - number // 4 - 1))
    mixed = jax.random.permutation(jax.random.fold_in(own, 3), amount)
    source_of, sink = mixed[0:amount // 2 * 2:2], mixed[1:amount // 2 * 2:2]
    slack = jnp.minimum(sizes[source_of] - 1, limit - sizes[sink]) // 2
    slack = jnp.where((source_of == ranking[0]) | (sink == ranking[0]) | (sizes[sink] == 0), 0, jnp.maximum(slack, 0))
    shifted = jax.random.randint(jax.random.fold_in(own, 4), (amount // 2,), 0, 1 << 20) % (slack + 1)
    sizes = sizes.at[source_of].add(-shifted).at[sink].add(shifted)
    members = jnp.searchsorted(jnp.cumsum(sizes), jnp.arange(rows * top), side="right").astype(jnp.int32)
    grid = members.reshape(top, rows).T
    grid = grid[jax.random.permutation(jax.random.fold_in(own, 1), rows)]
    offset_by = jax.random.randint(jax.random.fold_in(own, 2), (rows, 1), 0, top)
    return jnp.take_along_axis(grid, (jnp.arange(top)[None, :] + offset_by) % top, axis=1)


def load_shares(number_of, total, bound, slope, full):
    portions = [(1 << 20) // math.isqrt(grade ** slope) + 1 for grade in range(1, number_of + 1)]
    largest = bound if full else min(bound, max(-(-total // number_of), total * portions[0] // sum(portions)))
    least = 1 if total - largest >= number_of - 1 else 0
    holding, surplus = [largest] + [least] * (number_of - 1), total - largest - least * (number_of - 1)
    while surplus > 0:
        movable = [i for i in range(1, number_of) if holding[i] < largest] or [i for i in range(1, number_of) if holding[i] < bound]
        whole, remaining = sum([portions[i] for i in movable]), surplus
        for i in movable:
            addition = min(bound - holding[i], max(1, remaining * portions[i] // whole), surplus)
            holding[i] = holding[i] + addition
            surplus = surplus - addition
    return np.array(holding)


def bell_draw(own_key, shape, width, most, shards=(), held_as=jnp.bfloat16):
    values = jax.random.normal(own_key, shape, jnp.float32) * width
    if len(shards) > 0:
        values = steps_of(own_key, shape, shards, -0.22, 0.18) * values
    return jnp.clip(values, min=-most, max=most).astype(held_as)


def setup_inputs(seed: int = 0) -> dict:
    seeds = jax.random.split(jax.random.key(seed), 8)
    tokens = bell_draw(seeds[0], (TOKENS, D), 1.0, 6.0, ((0, 128), (1, 4)))
    grad_out = bell_draw(seeds[1], (TOKENS, D), 1.0, 6.0, ((0, 128), (1, 4)))
    expert_ids_keys = jax.random.split(jax.random.fold_in(seeds[2], 1), TOKENS // TOK_DEV)
    expert_ids_turns = jax.random.permutation(jax.random.fold_in(seeds[2], 3), TOKENS // TOK_DEV)
    expert_ids = jax.vmap(lambda own, number: assign_block(jax.random.fold_in(seeds[2], 2), own, number, TOK_DEV, EXPERTS, TOP, CAP, 2))(expert_ids_keys, expert_ids_turns).reshape((TOKENS, TOP))
    gate_scale = jnp.clip(jnp.exp(math.log(1.0) - 2.3025851 * jax.random.uniform(seeds[3], (TOKENS, TOP), jnp.float32) ** steps_of(seeds[3], (TOKENS, TOP), ((0, 128),), -0.2, 0.2)), 0.1, 1.0)
    gate_weight = bell_draw(seeds[4], (EXPERTS, F, D), D ** -0.5, 0.125, ((0, 128), (1, 4)))
    up_weight = bell_draw(seeds[5], (EXPERTS, F, D), D ** -0.5, 0.125, ((0, 128), (1, 4)))
    down_weight = bell_draw(seeds[6], (EXPERTS, F, D), F ** -0.5, 0.21875, ((0, 128), (2, 4)))
    return {"tokens": tokens, "grad_out": grad_out, "expert_ids": expert_ids, "gate_scale": gate_scale, "gate_weight": gate_weight, "up_weight": up_weight, "down_weight": down_weight}


def reference(tokens, grad_out, expert_ids, gate_scale, gate_weight, up_weight, down_weight):
    columns = TOKENS // TOK_DEV
    per_column = TOK_DEV * TOP
    column_ids = expert_ids.reshape(columns, per_column).astype(jnp.int32)
    onehot = (column_ids[:, :, None] == jnp.arange(EXPERTS, dtype=jnp.int32)[None, None, :]).astype(jnp.int32)
    ranks = jnp.sum((jnp.cumsum(onehot, axis=1) - 1) * onehot, axis=2).astype(jnp.int32)
    column_index = jnp.arange(columns, dtype=jnp.int32)[:, None]
    buffer_row = column_index * CAP + ranks
    token_index = column_index * TOK_DEV + jnp.arange(per_column, dtype=jnp.int32)[None, :] // TOP
    rows_total = columns * CAP
    flat_ids = column_ids.reshape(-1)
    flat_rows = buffer_row.reshape(-1)
    token_table = jnp.full((EXPERTS, rows_total), TOKENS, jnp.int32).at[flat_ids, flat_rows].set(token_index.reshape(-1).astype(jnp.int32))
    scale_table = jnp.zeros((EXPERTS, rows_total), jnp.float32).at[flat_ids, flat_rows].set(gate_scale.reshape(-1).astype(jnp.float32))
    padded_tokens = jnp.concatenate([tokens, jnp.zeros((1, D), tokens.dtype)], axis=0)
    padded_grad = jnp.concatenate([grad_out, jnp.zeros((1, D), grad_out.dtype)], axis=0)

    def one_expert(total, inputs):
        table_row, scale_row, gate_mat, up_mat, down_mat = inputs
        slot_tokens = padded_tokens[table_row]
        gate_pre = jnp.dot(slot_tokens, gate_mat.T, preferred_element_type=jnp.float32)
        up_pre = jnp.dot(slot_tokens, up_mat.T, preferred_element_type=jnp.float32)
        sigmoid_gate = jax.nn.sigmoid(gate_pre)
        activated = gate_pre * sigmoid_gate
        hidden = (activated * up_pre).astype(jnp.bfloat16)
        expert_out = jnp.dot(hidden, down_mat, preferred_element_type=jnp.float32).astype(jnp.bfloat16)
        total = total.at[table_row].add(scale_row[:, None] * expert_out.astype(jnp.float32))
        slot_grad = (scale_row[:, None] * padded_grad[table_row].astype(jnp.float32)).astype(jnp.bfloat16)
        hidden_grad = jnp.dot(slot_grad, down_mat.T, preferred_element_type=jnp.float32)
        gate_grad = (hidden_grad * up_pre * sigmoid_gate * (1.0 + gate_pre * (1.0 - sigmoid_gate))).astype(jnp.bfloat16)
        up_grad = (hidden_grad * activated).astype(jnp.bfloat16)
        down_out = jnp.dot(hidden.T, slot_grad, preferred_element_type=jnp.float32).astype(jnp.bfloat16)
        gate_out = jnp.dot(gate_grad.T, slot_tokens, preferred_element_type=jnp.float32).astype(jnp.bfloat16)
        up_out = jnp.dot(up_grad.T, slot_tokens, preferred_element_type=jnp.float32).astype(jnp.bfloat16)
        return total, (gate_out, up_out, down_out)

    start = jnp.zeros((TOKENS + 1, D), jnp.float32)
    total, grads = lax.scan(one_expert, start, (token_table, scale_table, gate_weight, up_weight, down_weight))
    return total[:TOKENS].astype(jnp.bfloat16), grads[0], grads[1], grads[2]
```

```python
import jax
import jax.numpy as jnp
from jax import lax
from jax.sharding import PartitionSpec as P


def slot_layout(route_ids, experts, capacity):
    flat_ids = route_ids.reshape(-1)
    onehot = (
        flat_ids[:, None] == lax.broadcasted_iota(jnp.int32, (flat_ids.shape[0], experts), 1)
    ).astype(jnp.int32)
    ranks = jnp.sum((jnp.cumsum(onehot, axis=0) - 1) * onehot, axis=1)
    return flat_ids * capacity + ranks


def place_matrix(positions, tok_rows, per_token, slots_total):
    slot_index = lax.broadcasted_iota(jnp.int32, (slots_total, tok_rows, per_token), 0)
    hits = slot_index == positions.reshape(1, tok_rows, per_token)
    return jnp.sum(hits.astype(jnp.float32), axis=2).astype(jnp.bfloat16)


def send_rows(outgoing):
    return lax.all_to_all(outgoing, ("grp", "loc"), split_axis=0, concat_axis=0, tiled=True)


def return_rows(results):
    return lax.all_to_all(results, ("grp", "loc"), split_axis=0, concat_axis=0, tiled=True)


def body(tokens, grad_out, expert_ids, gate_scale, gate_weight, up_weight, down_weight):
    tok_rows, quarter = tokens.shape
    per_token = expert_ids.shape[1]
    experts = lax.axis_size(("grp", "loc"))
    capacity = min(tok_rows, max(2, 2 * tok_rows * per_token // experts))
    slots_total = experts * capacity
    positions = slot_layout(expert_ids, experts, capacity)
    unit_place = place_matrix(positions, tok_rows, per_token, slots_total)
    slot_scale = jnp.zeros((slots_total,), jnp.float32).at[positions].set(gate_scale.reshape(-1))
    picked_grads = jnp.dot(unit_place, grad_out, preferred_element_type=jnp.float32)
    grad_rows = (picked_grads * slot_scale[:, None]).astype(jnp.bfloat16)
    token_rows = jnp.dot(unit_place, tokens, preferred_element_type=jnp.float32).astype(
        jnp.bfloat16
    )
    outgoing = jnp.concatenate([token_rows, grad_rows], axis=1).reshape(
        experts, capacity, 2 * quarter
    )
    arrived = send_rows(outgoing).reshape(slots_total, 2 * quarter)
    flat_grads = arrived[:, quarter:]
    flat_tokens = lax.all_gather(arrived[:, :quarter], "dp", axis=1, tiled=True)
    gate_mat = gate_weight[0]
    up_mat = up_weight[0]
    down_mat = down_weight[0]
    feature_contract = (((1,), (1,)), ((), ()))
    gate_pre = lax.dot_general(
        gate_mat, flat_tokens, feature_contract, preferred_element_type=jnp.float32
    )
    up_pre = lax.dot_general(
        up_mat, flat_tokens, feature_contract, preferred_element_type=jnp.float32
    )
    sigmoid_gate = jax.nn.sigmoid(gate_pre)
    activated = gate_pre * sigmoid_gate
    hidden = (activated * up_pre).astype(jnp.bfloat16)
    piece = lax.all_gather(hidden, "dp", axis=0, tiled=True)
    down_rows = down_mat
    out_total = lax.dot_general(
        piece, down_rows, (((0,), (0,)), ((), ())), preferred_element_type=jnp.float32
    )
    block_grad = jnp.dot(piece, flat_grads, preferred_element_type=jnp.float32)
    down_total = block_grad
    out_total, down_total = (out_total, down_total)
    expert_out = out_total.astype(jnp.bfloat16)
    down_gradient = down_total.astype(jnp.bfloat16)
    returned = return_rows(expert_out.reshape(experts, capacity, quarter)).reshape(
        slots_total, quarter
    )
    picked = returned[positions].astype(jnp.float32) * gate_scale.reshape(-1)[:, None]
    layer_out = jnp.sum(picked.reshape(tok_rows, per_token, quarter), axis=1).astype(jnp.bfloat16)
    down_rows = down_mat
    hidden_grad = lax.psum_scatter(
        lax.dot_general(
            down_rows, flat_grads, feature_contract, preferred_element_type=jnp.float32
        ),
        "dp",
        scatter_dimension=0,
        tiled=True,
    )
    gate_grad = (
        hidden_grad * up_pre * sigmoid_gate * (1.0 + gate_pre * (1.0 - sigmoid_gate))
    ).astype(jnp.bfloat16)
    up_grad = (hidden_grad * activated).astype(jnp.bfloat16)
    gate_gradient = jnp.dot(gate_grad, flat_tokens, preferred_element_type=jnp.float32).astype(
        jnp.bfloat16
    )
    up_gradient = jnp.dot(up_grad, flat_tokens, preferred_element_type=jnp.float32).astype(
        jnp.bfloat16
    )
    return (layer_out, gate_gradient[None], up_gradient[None], down_gradient[None])


def solution(mesh):
    return jax.shard_map(
        body,
        mesh=mesh,
        in_specs=(
            P(("grp", "loc"), "dp"),
            P(("grp", "loc"), "dp"),
            P(("grp", "loc"), None),
            P(("grp", "loc"), None),
            P(("grp", "loc"), "dp", None),
            P(("grp", "loc"), "dp", None),
            P(("grp", "loc"), None, "dp"),
        ),
        out_specs=(
            P(("grp", "loc"), "dp"),
            P(("grp", "loc"), "dp", None),
            P(("grp", "loc"), "dp", None),
            P(("grp", "loc"), None, "dp"),
        ),
        check_vma=False,
    )
```

```python
import functools

import jax
import jax.numpy as jnp
from jax import lax
from jax.experimental import pallas as pl
from jax.experimental.pallas import tpu as pltpu
from jax.sharding import PartitionSpec as P

MESH = pl.DeviceIdType.MESH
CAP = 8
PAIR = 2 * CAP


def slot_layout(route_ids, experts, capacity):
    flat_ids = route_ids.reshape(-1)
    onehot = (
        flat_ids[:, None] == lax.broadcasted_iota(jnp.int32, (flat_ids.shape[0], experts), 1)
    ).astype(jnp.int32)
    ranks = jnp.sum((jnp.cumsum(onehot, axis=0) - 1) * onehot, axis=1)
    return flat_ids * capacity + ranks


def route_rows(ids, scale, plane_experts, planes):
    rows, per_token = ids.shape
    experts = plane_experts * planes
    expert_lane = lax.broadcasted_iota(jnp.int32, (rows, experts), 1)
    hits = [ids[:, k : k + 1] == expert_lane for k in range(per_token)]
    named = sum(h.astype(jnp.float32) for h in hits).astype(jnp.bfloat16)
    row_at = lax.broadcasted_iota(jnp.int32, (rows, rows), 0)
    col_at = lax.broadcasted_iota(jnp.int32, (rows, rows), 1)
    earlier = (col_at < row_at).astype(jnp.float32).astype(jnp.bfloat16)
    before = jnp.dot(earlier, named, preferred_element_type=jnp.float32)
    lane = lax.broadcasted_iota(jnp.int32, (rows, rows), 1)
    table = jnp.zeros((rows, rows), jnp.float32)
    loc_size = 2 * planes
    for k in range(per_token):
        rank = jnp.sum(jnp.where(hits[k], before, 0.0), axis=1, keepdims=True)
        e = ids[:, k : k + 1]
        group = lax.div(e, jnp.int32(loc_size))
        local = e - group * loc_size
        plane = lax.div(local, jnp.int32(2))
        member = group * 2 + (local - plane * 2)
        key = (plane * (plane_experts * PAIR) + member * PAIR).astype(jnp.float32) + rank
        table = jnp.where(lane == k, key, table)
        table = jnp.where(lane == per_token + k, scale[:, k : k + 1], table)
    return table.T[0 : 2 * per_token, :]


def dispatch_kernel(
    nx, nz, ids_ref, scale_ref, tok_ref, grad_ref, otok_ref, ograd_ref,
    zt, zg, zm, xt, xg, slot_t, slot_g,
    z_send, z_recv, x_send, x_recv, y_send, y_recv, l_sem,
):
    R = nz // 2
    J = 2 * nx
    per_token = ids_ref.shape[1]
    y = lax.axis_index("dp")
    x = lax.axis_index("grp")
    loc = lax.axis_index("loc")
    z = loc // 2
    core = loc % 2
    me = x * 2 + core
    z_right = {"loc": ((z + 1) % nz) * 2 + core}
    z_left = {"loc": ((z + nz - 1) % nz) * 2 + core}
    yp, ym, yo = (y + 1) % 4, (y + 3) % 4, (y + 2) % 4
    y_up, y_down = {"dp": yp}, {"dp": ym}

    def plane_device(j):
        return {"grp": j // 2, "loc": z * 2 + j % 2}

    barrier = pltpu.get_barrier_semaphore()
    greeted = [z_right, z_left, y_up, y_down]
    greeted += [plane_device((me + o) % J) for o in range(1, J)]
    for device in greeted:
        pl.semaphore_signal(barrier, inc=1, device_id=device, device_id_type=MESH)

    zt[0, 0] = tok_ref[...]
    zg[0, 0] = grad_ref[...]
    zm[0, 0] = route_rows(ids_ref[...], scale_ref[...], J, nz)
    pl.semaphore_wait(barrier, len(greeted))

    bufs = (zt, zg, zm)

    def z_copy(kind, way, step, src, dst):
        return pltpu.make_async_remote_copy(
            src_ref=bufs[kind].at[src],
            dst_ref=bufs[kind].at[dst],
            send_sem=z_send.at[way, step, kind],
            recv_sem=z_recv.at[dst[0], dst[1], kind],
            device_id=z_right if way == 0 else z_left,
            device_id_type=MESH,
        )

    def x_copy(kind, i, o):
        j = (me + o) % J
        src, dst = ((xt, slot_t.at[y]), (xg, slot_g))[kind]
        return pltpu.make_async_remote_copy(
            src_ref=src.at[i, j],
            dst_ref=dst.at[i, me],
            send_sem=x_send.at[i, kind, o],
            recv_sem=x_recv.at[i, kind, o],
            device_id=plane_device(j),
            device_id_type=MESH,
        )

    def x_own(kind, i):
        src, dst = ((xt, slot_t.at[y]), (xg, slot_g))[kind]
        return pltpu.make_async_copy(src.at[i, me], dst.at[i, me], x_recv.at[i, kind, 0])

    def y_copy(k, i):
        ref = (
            slot_t.at[y, i],
            slot_t.at[y, i],
            slot_t.at[ym, i, pl.ds(0, J // 2)],
            slot_t.at[yp, i, pl.ds(J // 2, J // 2)],
        )[k]
        return pltpu.make_async_remote_copy(
            src_ref=ref,
            dst_ref=ref,
            send_sem=y_send.at[i, k],
            recv_sem=y_recv.at[i, k],
            device_id=y_up if k % 2 == 0 else y_down,
            device_id_type=MESH,
        )

    def y_arrival(k, i):
        ref = (
            slot_t.at[ym, i],
            slot_t.at[yp, i],
            slot_t.at[yo, i, pl.ds(0, J // 2)],
            slot_t.at[yo, i, pl.ds(J // 2, J // 2)],
        )[k]
        return pltpu.make_async_remote_copy(
            src_ref=ref,
            dst_ref=ref,
            send_sem=y_send.at[i, k],
            recv_sem=y_recv.at[i, k],
            device_id=y_up if k % 2 == 0 else y_down,
            device_id_type=MESH,
        )

    def select(i):
        marks, weights = [], 0.0
        for h in range(2):
            row_key = (
                lax.broadcasted_iota(jnp.int32, (J * PAIR, zm.shape[3]), 0)
                + (z * (J * PAIR) - h * CAP)
            ).astype(jnp.float32)
            table = zm[i, h]
            mark = 0.0
            for k in range(per_token):
                hit = table[k : k + 1, :] == row_key
                mark = mark + jnp.where(hit, 1.0, 0.0)
                weights = weights + jnp.where(hit, table[per_token + k : per_token + k + 1, :], 0.0)
            marks.append(mark)
        place = jnp.concatenate(marks, axis=1).astype(jnp.bfloat16)
        row_scale = jnp.sum(weights, axis=1, keepdims=True)
        Q = zt.shape[3]
        picked = jnp.dot(
            place, zt[i].reshape(-1, Q), preferred_element_type=jnp.float32
        )
        xt[i] = picked.astype(jnp.bfloat16).reshape(J, PAIR, Q)
        picked_g = jnp.dot(
            place, zg[i].reshape(-1, Q), preferred_element_type=jnp.float32
        )
        xg[i] = (picked_g * row_scale).astype(jnp.bfloat16).reshape(J, PAIR, Q)

    def z_stage(i):
        @pl.when(i >= 1)
        def _():
            for kind in (0, 2):
                z_copy(kind, 1, 0, (i, 0), (i, 0)).wait_recv()

        @pl.when(i < R - 1)
        def _():
            for kind in (0, 2):
                z_copy(kind, 1, i, (i, 0), (i + 1, 0)).start()

        for kind in (0, 2):
            z_copy(kind, 0, 0, (i, 1), (i, 1)).wait_recv()

        @pl.when(i < R - 1)
        def _():
            for kind in (0, 2):
                z_copy(kind, 0, i + 1, (i, 1), (i + 1, 1)).start()

        @pl.when(i >= 1)
        def _():
            z_copy(1, 1, 0, (i, 0), (i, 0)).wait_recv()

        @pl.when(i < R - 1)
        def _():
            z_copy(1, 1, i, (i, 0), (i + 1, 0)).start()

        @pl.when(i == R - 1)
        def _():
            z_copy(1, 1, R - 1, (R - 1, 0), (R - 1, 1)).start()

        z_copy(1, 0, 0, (i, 1), (i, 1)).wait_recv()

        @pl.when(i < R - 2)
        def _():
            z_copy(1, 0, i + 1, (i, 1), (i + 1, 1)).start()

        select(i)
        for kind in (0, 1):
            x_own(kind, i).start()
            for o in range(1, J):
                x_copy(kind, i, o).start()

    def x_arrival(kind, i, o):
        src, dst = ((xt, slot_t.at[y]), (xg, slot_g))[kind]
        return pltpu.make_async_remote_copy(
            src_ref=src.at[i, 0],
            dst_ref=dst.at[i, (me + J - o) % J],
            send_sem=x_send.at[i, kind, o],
            recv_sem=x_recv.at[i, kind, o],
            device_id=plane_device((me + o) % J),
            device_id_type=MESH,
        )

    def x_stage(i):
        x_own(0, i).wait()
        for o in range(1, J):
            x_arrival(0, i, o).wait_recv()
        y_copy(0, i).start()
        y_copy(1, i).start()
        x_own(1, i).wait()
        for o in range(1, J):
            x_arrival(1, i, o).wait_recv()

    def y_stage(i):
        y_arrival(0, i).wait_recv()
        y_copy(2, i).start()
        y_arrival(1, i).wait_recv()
        y_copy(3, i).start()

    def last_stage(i):
        y_arrival(2, i).wait_recv()
        y_arrival(3, i).wait_recv()

    for kind in (0, 2, 1):
        if kind == 1 and R == 1:
            continue
        z_copy(kind, 0, 0, (0, 0), (0, 1)).start()

    def step(i, carry):
        @pl.when(i < R)
        def _():
            z_stage(i)

        @pl.when((i >= 1) & (i < R + 1))
        def _():
            x_stage(i - 1)

        @pl.when((i >= 2) & (i < R + 2))
        def _():
            y_stage(i - 2)

        @pl.when(i >= 3)
        def _():
            last_stage(i - 3)

        return carry

    lax.fori_loop(0, R + 3, step, 0)

    out_t = pltpu.make_async_copy(slot_t, otok_ref, l_sem.at[0])
    out_g = pltpu.make_async_copy(slot_g, ograd_ref, l_sem.at[1])
    out_t.start()
    out_g.start()

    def drain(i, carry):
        for kind in (0, 2):
            z_copy(kind, 0, i, (0, 0), (0, 1)).wait_send()

        @pl.when(i < R - 1)
        def _():
            z_copy(1, 0, i, (0, 0), (0, 1)).wait_send()
            for kind in (0, 2):
                z_copy(kind, 1, i, (0, 0), (0, 1)).wait_send()

        z_copy(1, 1, i, (0, 0), (0, 1)).wait_send()
        for kind in (0, 1):
            for o in range(1, J):
                x_copy(kind, i, o).wait_send()
        for k in range(4):
            y_copy(k, i).wait_send()
        return carry

    lax.fori_loop(0, R, drain, 0)
    out_t.wait()
    out_g.wait()


def dispatch(ids, scale, tokens, grad_out):
    nx = lax.axis_size("grp")
    nz = lax.axis_size("loc") // 2
    rows, Q = tokens.shape
    R, J = nz // 2, 2 * nx
    bf16 = jnp.bfloat16
    vmem = pl.BlockSpec(memory_space=pltpu.VMEM)
    hbm = pl.BlockSpec(memory_space=pl.ANY)
    return pl.pallas_call(
        functools.partial(dispatch_kernel, nx, nz),
        out_shape=(
            jax.ShapeDtypeStruct((4, R, J, PAIR, Q), bf16),
            jax.ShapeDtypeStruct((R, J, PAIR, Q), bf16),
        ),
        in_specs=[vmem] * 4,
        out_specs=(hbm, hbm),
        scratch_shapes=[
            pltpu.VMEM((R, 2, rows, Q), bf16),
            pltpu.VMEM((R, 2, rows, Q), bf16),
            pltpu.VMEM((R, 2, 2 * ids.shape[1], rows), jnp.float32),
            pltpu.VMEM((R, J, PAIR, Q), bf16),
            pltpu.VMEM((R, J, PAIR, Q), bf16),
            pltpu.VMEM((4, R, J, PAIR, Q), bf16),
            pltpu.VMEM((R, J, PAIR, Q), bf16),
            pltpu.SemaphoreType.DMA((2, R, 3)),
            pltpu.SemaphoreType.DMA((R, 2, 3)),
            pltpu.SemaphoreType.DMA((R, 2, J)),
            pltpu.SemaphoreType.DMA((R, 2, J)),
            pltpu.SemaphoreType.DMA((R, 4)),
            pltpu.SemaphoreType.DMA((R, 4)),
            pltpu.SemaphoreType.DMA((2,)),
        ],
        compiler_params=pltpu.CompilerParams(
            collective_id=0, has_side_effects=True, vmem_limit_bytes=40 * 1024 * 1024
        ),
    )(ids, scale, tokens, grad_out)


def body(tokens, grad_out, expert_ids, gate_scale, gate_weight, up_weight, down_weight):
    tok_rows, quarter = tokens.shape
    per_token = expert_ids.shape[1]
    experts = lax.axis_size(("grp", "loc"))
    nx = lax.axis_size("grp")
    nz = lax.axis_size("loc") // 2
    R, J = nz // 2, 2 * nx
    slots_total = experts * CAP
    positions = slot_layout(expert_ids, experts, CAP)
    slot_t, slot_g = dispatch(expert_ids, gate_scale, tokens, grad_out)
    flat_tokens = jnp.concatenate(
        [slot_t[q].reshape(slots_total, quarter) for q in range(4)], axis=1
    )
    flat_grads = slot_g.reshape(slots_total, quarter)
    gate_mat = gate_weight[0]
    up_mat = up_weight[0]
    down_mat = down_weight[0]
    feature_contract = (((1,), (1,)), ((), ()))
    gate_pre = lax.dot_general(
        gate_mat, flat_tokens, feature_contract, preferred_element_type=jnp.float32
    )
    up_pre = lax.dot_general(
        up_mat, flat_tokens, feature_contract, preferred_element_type=jnp.float32
    )
    sigmoid_gate = jax.nn.sigmoid(gate_pre)
    activated = gate_pre * sigmoid_gate
    hidden = (activated * up_pre).astype(jnp.bfloat16)
    piece = lax.all_gather(hidden, "dp", axis=0, tiled=True)
    out_total = lax.dot_general(
        piece, down_mat, (((0,), (0,)), ((), ())), preferred_element_type=jnp.float32
    )
    block_grad = jnp.dot(piece, flat_grads, preferred_element_type=jnp.float32)
    expert_out = out_total.astype(jnp.bfloat16)
    down_gradient = block_grad.astype(jnp.bfloat16)
    z = lax.axis_index("loc") // 2
    by_round = expert_out.reshape(R, J, 2, CAP, quarter)
    by_delta = jnp.concatenate([by_round[:, :, 0], by_round[::-1, :, 1]], axis=0)
    order = (jnp.arange(nz) - z) % nz
    by_plane = by_delta[order].reshape(nz, nx, 2, CAP, quarter).transpose(1, 0, 2, 3, 4)
    returned = lax.all_to_all(
        by_plane.reshape(experts, CAP, quarter), ("grp", "loc"), 0, 0, tiled=True
    ).reshape(slots_total, quarter)
    picked = returned[positions].astype(jnp.float32) * gate_scale.reshape(-1)[:, None]
    layer_out = jnp.sum(picked.reshape(tok_rows, per_token, quarter), axis=1).astype(jnp.bfloat16)
    hidden_grad = lax.psum_scatter(
        lax.dot_general(
            down_mat, flat_grads, feature_contract, preferred_element_type=jnp.float32
        ),
        "dp",
        scatter_dimension=0,
        tiled=True,
    )
    gate_grad = (
        hidden_grad * up_pre * sigmoid_gate * (1.0 + gate_pre * (1.0 - sigmoid_gate))
    ).astype(jnp.bfloat16)
    up_grad = (hidden_grad * activated).astype(jnp.bfloat16)
    gate_gradient = jnp.dot(gate_grad, flat_tokens, preferred_element_type=jnp.float32).astype(
        jnp.bfloat16
    )
    up_gradient = jnp.dot(up_grad, flat_tokens, preferred_element_type=jnp.float32).astype(
        jnp.bfloat16
    )
    return (layer_out, gate_gradient[None], up_gradient[None], down_gradient[None])


def solution(mesh):
    return jax.shard_map(
        body,
        mesh=mesh,
        in_specs=(
            P(("grp", "loc"), "dp"),
            P(("grp", "loc"), "dp"),
            P(("grp", "loc"), None),
            P(("grp", "loc"), None),
            P(("grp", "loc"), "dp", None),
            P(("grp", "loc"), "dp", None),
            P(("grp", "loc"), None, "dp"),
        ),
        out_specs=(
            P(("grp", "loc"), "dp"),
            P(("grp", "loc"), "dp", None),
            P(("grp", "loc"), "dp", None),
            P(("grp", "loc"), None, "dp"),
        ),
        check_vma=False,
    )
```

```python
import functools

import jax
import jax.numpy as jnp
from jax import lax
from jax.experimental import pallas as pl
from jax.experimental.pallas import tpu as pltpu
from jax.sharding import PartitionSpec as P

MESH = pl.DeviceIdType.MESH
CAP = 8
PAIR = 2 * CAP
BF16 = jnp.bfloat16
F32 = jnp.float32
NT = (((1,), (1,)), ((), ()))
TN = (((0,), (0,)), ((), ()))


def dot(a, b, dims=(((1,), (0,)), ((), ()))):
    return lax.dot_general(a, b, dims, preferred_element_type=F32)


def route_keys(ids, experts, planes):
    per_token, rows = ids.shape
    expert_row = lax.broadcasted_iota(jnp.int32, (experts, rows), 0)
    hits = [ids[k : k + 1, :] == expert_row for k in range(per_token)]
    named = sum(jnp.where(h, 1.0, 0.0) for h in hits).astype(BF16)
    row_at = lax.broadcasted_iota(jnp.int32, (rows, rows), 0)
    col_at = lax.broadcasted_iota(jnp.int32, (rows, rows), 1)
    before = dot(named, jnp.where(row_at < col_at, 1.0, 0.0).astype(BF16))
    ranks = jnp.concatenate(
        [jnp.sum(jnp.where(h, before, 0.0), axis=0, keepdims=True) for h in hits], axis=0
    )
    group = lax.div(ids, jnp.int32(2 * planes))
    local = ids - group * (2 * planes)
    plane = lax.div(local, jnp.int32(2))
    member = group * 2 + (local - plane * 2)
    return plane, member, ranks


def layer_kernel(
    nx, nz,
    ids_hbm, scale_hbm, tok_hbm, grad_hbm, gate_hbm, up_hbm, down_hbm,
    layer_out, gate_out, up_out, down_out,
    ids_v, scale_v, wv, dv,
    zt, zg, zm, xt, xg, slot_t, slot_g,
    pre, hid, hgp, rs_a, rs_b, rs_c, rs_d,
    eo, rx, rz, fin, grads, wout, dout, lout, place_v,
    l_sem, z_send, z_recv, x_send, x_recv, y_send, y_recv, h_send, h_recv,
    s_send, s_recv, e_send, e_recv, f_send, f_recv,
):
    R = nz // 2
    J = 2 * nx
    per_token = ids_v.shape[0]
    Q = zt.shape[3]
    F = hid.shape[2]
    S = J * PAIR
    C = J * CAP
    y = lax.axis_index("dp")
    x = lax.axis_index("grp")
    loc = lax.axis_index("loc")
    z = loc // 2
    core = loc % 2
    me = x * 2 + core
    yp, ym, yo = (y + 1) % 4, (y + 3) % 4, (y + 2) % 4
    y_up, y_down = {"dp": yp}, {"dp": ym}

    def at_plane(p):
        return {"loc": (p % nz) * 2 + core}

    def member_at(j):
        return {"grp": j // 2, "loc": z * 2 + j % 2}

    z_right, z_left = at_plane(z + 1), at_plane(z + nz - 1)

    barrier = pltpu.get_barrier_semaphore()
    greeted = [at_plane(z + d) for d in range(1, nz)] + [y_up, y_down]
    greeted += [member_at((me + o) % J) for o in range(1, J)]
    for device in greeted:
        pl.semaphore_signal(barrier, inc=1, device_id=device, device_id_type=MESH)

    loads = [
        pltpu.make_async_copy(src, dst, l_sem.at[n])
        for n, (src, dst) in enumerate(
            [
                (ids_hbm, ids_v),
                (scale_hbm, scale_v),
                (tok_hbm, zt.at[0, 0]),
                (grad_hbm, zg.at[0, 0]),
                (gate_hbm, wv.at[0]),
                (up_hbm, wv.at[1]),
                (down_hbm, dv),
            ]
        )
    ]
    for load in loads:
        load.start()
    loads[0].wait()
    loads[1].wait()
    plane, member, ranks = route_keys(ids_v[...], nz * J, nz)
    scales = scale_v[...]
    zm[0, 0] = jnp.concatenate(
        [(plane * S + member * PAIR).astype(F32) + ranks, scales], axis=0
    )
    loads[2].wait()
    loads[3].wait()
    pl.semaphore_wait(barrier, len(greeted))

    bufs = (zt, zg, zm)

    def z_copy(kind, way, step, src, dst):
        return pltpu.make_async_remote_copy(
            src_ref=bufs[kind].at[src],
            dst_ref=bufs[kind].at[dst],
            send_sem=z_send.at[way, step, kind],
            recv_sem=z_recv.at[dst[0], dst[1], kind],
            device_id=z_right if way == 0 else z_left,
            device_id_type=MESH,
        )

    def member_copy(src, dst, sems, i, o, j):
        send, recv = sems
        return pltpu.make_async_remote_copy(
            src_ref=src,
            dst_ref=dst,
            send_sem=send.at[i, o],
            recv_sem=recv.at[i, o],
            device_id=member_at(j),
            device_id_type=MESH,
        )

    def exchange(kind):
        return (
            (xt, slot_t.at[y], (x_send.at[0], x_recv.at[0])),
            (xg, slot_g, (x_send.at[1], x_recv.at[1])),
            (eo, rx, (e_send, e_recv)),
        )[kind]

    def exchange_own(kind, i):
        src, dst, sems = exchange(kind)
        return pltpu.make_async_copy(src.at[i, me], dst.at[i, me], sems[1].at[i, 0])

    def exchange_copy(kind, i, o):
        src, dst, sems = exchange(kind)
        j = (me + o) % J
        return member_copy(src.at[i, j], dst.at[i, me], sems, i, o, j)

    def exchange_arrival(kind, i, o):
        src, dst, sems = exchange(kind)
        return member_copy(
            src.at[i, 0], dst.at[i, (me + J - o) % J], sems, i, o, (me + o) % J
        )

    def exchange_start(kind, i):
        exchange_own(kind, i).start()
        for o in range(1, J):
            exchange_copy(kind, i, o).start()

    def exchange_wait(kind, i):
        exchange_own(kind, i).wait()
        for o in range(1, J):
            exchange_arrival(kind, i, o).wait_recv()

    def dp_copy(ref, dst, send, recv, up):
        return pltpu.make_async_remote_copy(
            src_ref=ref,
            dst_ref=dst,
            send_sem=send,
            recv_sem=recv,
            device_id=y_up if up else y_down,
            device_id_type=MESH,
        )

    def gather(kind, k, i, arrival=False):
        buf, half, send, recv = (
            (slot_t, J // 2, y_send, y_recv),
            (hid, F // 2, h_send, h_recv),
        )[kind]
        lower, upper = pl.ds(0, half), pl.ds(half, half)
        if arrival:
            ref = (buf.at[ym, i], buf.at[yp, i], buf.at[yo, i, lower], buf.at[yo, i, upper])[k]
        else:
            ref = (buf.at[y, i], buf.at[y, i], buf.at[ym, i, lower], buf.at[yp, i, upper])[k]
        return dp_copy(ref, ref, send.at[i, k], recv.at[i, k], k % 2 == 0)

    def reduce(k, i):
        half = F // 2
        lower, upper = pl.ds(0, half), pl.ds(half, half)
        src = (hgp.at[i, yo, lower], hgp.at[i, yo, upper], hgp.at[i, yp], hgp.at[i, ym])[k]
        dst = (rs_a, rs_b, rs_c, rs_d)[k].at[i]
        return dp_copy(src, dst, s_send.at[i, k], s_recv.at[i, k], k % 2 == 0)

    def return_copy(h, i):
        return pltpu.make_async_remote_copy(
            src_ref=rz.at[i, h],
            dst_ref=fin.at[i, h],
            send_sem=f_send.at[i, h],
            recv_sem=f_recv.at[i, h],
            device_id=at_plane(z + i) if h == 0 else at_plane(z + nz - i - 1),
            device_id_type=MESH,
        )

    def return_own():
        return pltpu.make_async_copy(rz.at[0, 0], fin.at[0, 0], f_recv.at[0, 0])

    def select(i):
        marks, weights = [], 0.0
        for h in range(2):
            row_key = (
                lax.broadcasted_iota(jnp.int32, (S, zm.shape[3]), 0) + (z * S - h * CAP)
            ).astype(F32)
            table = zm[i, h]
            mark = 0.0
            for k in range(per_token):
                hit = table[k : k + 1, :] == row_key
                mark = mark + jnp.where(hit, 1.0, 0.0)
                weights = weights + jnp.where(hit, table[per_token + k : per_token + k + 1, :], 0.0)
            marks.append(mark)
        place = jnp.concatenate(marks, axis=1).astype(BF16)
        row_scale = jnp.sum(weights, axis=1, keepdims=True)
        xt[i] = dot(place, zt[i].reshape(-1, Q)).astype(BF16).reshape(J, PAIR, Q)
        xg[i] = (dot(place, zg[i].reshape(-1, Q)) * row_scale).astype(BF16).reshape(J, PAIR, Q)

    def z_stage(i):
        @pl.when(i >= 1)
        def _():
            for kind in (0, 2):
                z_copy(kind, 1, 0, (i, 0), (i, 0)).wait_recv()

        @pl.when(i < R - 1)
        def _():
            for kind in (0, 2):
                z_copy(kind, 1, i, (i, 0), (i + 1, 0)).start()

        for kind in (0, 2):
            z_copy(kind, 0, 0, (i, 1), (i, 1)).wait_recv()

        @pl.when(i < R - 1)
        def _():
            for kind in (0, 2):
                z_copy(kind, 0, i + 1, (i, 1), (i + 1, 1)).start()

        @pl.when(i >= 1)
        def _():
            z_copy(1, 1, 0, (i, 0), (i, 0)).wait_recv()

        @pl.when(i < R - 1)
        def _():
            z_copy(1, 1, i, (i, 0), (i + 1, 0)).start()

        @pl.when(i == R - 1)
        def _():
            z_copy(1, 1, R - 1, (R - 1, 0), (R - 1, 1)).start()

        z_copy(1, 0, 0, (i, 1), (i, 1)).wait_recv()

        @pl.when(i < R - 2)
        def _():
            z_copy(1, 0, i + 1, (i, 1), (i + 1, 1)).start()

        select(i)
        exchange_start(0, i)
        exchange_start(1, i)

    def x_stage(i):
        exchange_wait(0, i)
        gather(0, 0, i).start()
        gather(0, 1, i).start()
        exchange_wait(1, i)

    def relay_stage(kind, i):
        for k in range(2):
            gather(kind, k, i, True).wait_recv()
            gather(kind, k + 2, i).start()

    def relay_wait(kind, i):
        gather(kind, 2, i, True).wait_recv()
        gather(kind, 3, i, True).wait_recv()

    def hidden_stage(i):
        relay_wait(0, i)
        rows = jnp.concatenate([slot_t[q, i].reshape(S, Q) for q in range(4)], axis=1)
        both = dot(wv[...].reshape(2 * F, 4 * Q), rows, NT)
        pre[i] = both
        g, u = both[0:F], both[F : 2 * F]
        hid[y, i] = (g * jax.nn.sigmoid(g) * u).astype(BF16)
        gather(1, 0, i).start()
        gather(1, 1, i).start()

    def down_stage(i):
        relay_wait(1, i)
        total = dot(hid[:, i].reshape(4 * F, S), dv[...], TN)
        eo[i] = total.astype(BF16).reshape(J, PAIR, Q)
        exchange_start(2, i)

    def return_stage(i):
        exchange_wait(2, i)
        row = lax.broadcasted_iota(jnp.int32, (S, S), 0)
        col = lax.broadcasted_iota(jnp.int32, (S, S), 1)
        h = lax.div(row, jnp.int32(C))
        j = lax.div(row - h * C, jnp.int32(CAP))
        source = j * PAIR + h * CAP + (row - h * C - j * CAP)
        swap = jnp.where(col == source, 1.0, 0.0).astype(BF16)
        rz[i] = dot(swap, rx[i].reshape(S, Q)).astype(BF16).reshape(2, C, Q)

        @pl.when(i >= 1)
        def _():
            return_copy(0, i).start()

        @pl.when(i == 0)
        def _():
            return_own().start()

        return_copy(1, i).start()

    def sum_first(i):
        part = dot(dv[...], slot_g[i].reshape(S, Q), NT)
        hgp[i] = part.reshape(4, F, S)
        reduce(0, i).start()
        reduce(1, i).start()

    def sum_second(i):
        half = F // 2
        reduce(0, i).wait_recv()
        hgp[i, yp, 0:half] = hgp[i, yp, 0:half] + rs_a[i]
        reduce(2, i).start()
        reduce(1, i).wait_recv()
        hgp[i, ym, half:F] = hgp[i, ym, half:F] + rs_b[i]
        reduce(3, i).start()

    def sum_last(i):
        reduce(2, i).wait_recv()
        reduce(3, i).wait_recv()
        hidden_grad = hgp[i, y] + rs_c[i] + rs_d[i]
        g, u = pre[i, 0:F], pre[i, F : 2 * F]
        s = jax.nn.sigmoid(g)
        gate_grad = hidden_grad * u * s * (1.0 + g * (1.0 - s))
        up_grad = hidden_grad * (g * s)
        grads[i] = jnp.concatenate([gate_grad, up_grad], axis=0).astype(BF16)

    for kind in (0, 2, 1):
        z_copy(kind, 0, 0, (0, 0), (0, 1)).start()

    delta = z - plane
    delta = jnp.where(delta < 0, delta + nz, delta)
    back = jnp.where(delta < R, delta * 2, (nz - 1 - delta) * 2 + 1)
    row_of = (back * C + member * CAP).astype(F32) + ranks
    packed = jnp.concatenate([row_of, scales], axis=0)
    tokens = packed.shape[1]
    packed = jnp.concatenate(
        [packed, jnp.zeros((tokens - 2 * per_token, tokens), F32)], axis=0
    ).T
    for r in range(R):
        lane = (lax.broadcasted_iota(jnp.int32, (tokens, 2 * C), 1) + r * 2 * C).astype(F32)
        weight = 0.0
        for k in range(per_token):
            hit = packed[:, k : k + 1] == lane
            weight = weight + jnp.where(hit, packed[:, per_token + k : per_token + k + 1], 0.0)
        for part in range(3):
            piece = weight.astype(BF16)
            place_v[part, :, r * 2 * C : (r + 1) * 2 * C] = piece
            weight = weight - piece.astype(F32)
    for load in loads[4:]:
        load.wait()

    stages = (
        (0, z_stage),
        (1, x_stage),
        (2, functools.partial(relay_stage, 0)),
        (3, hidden_stage),
        (4, functools.partial(relay_stage, 1)),
        (5, down_stage),
        (6, return_stage),
        (6, sum_first),
        (7, sum_second),
        (8, sum_last),
    )

    def step(i, carry):
        for lag, stage in stages:

            @pl.when((i >= lag) & (i < R + lag))
            def _(lag=lag, stage=stage):
                stage(i - lag)

        return carry

    lax.fori_loop(0, R + 8, step, 0)

    flat_g = slot_g[...].reshape(R * S, Q)
    for q in range(4):
        lhs = jnp.concatenate([hid[q, r] for r in range(R)], axis=1)
        dout[q * F : (q + 1) * F] = dot(lhs, flat_g).astype(BF16)
    stores = [pltpu.make_async_copy(dout, down_out, l_sem.at[0])]
    stores[0].start()
    lhs = jnp.concatenate([grads[r] for r in range(R)], axis=1)
    for q in range(4):
        res = dot(lhs, slot_t[q].reshape(R * S, Q)).astype(BF16)
        wout[0, :, q * Q : (q + 1) * Q] = res[0:F]
        wout[1, :, q * Q : (q + 1) * Q] = res[F : 2 * F]
    stores.append(pltpu.make_async_copy(wout.at[0], gate_out, l_sem.at[1]))
    stores.append(pltpu.make_async_copy(wout.at[1], up_out, l_sem.at[2]))
    stores[1].start()
    stores[2].start()

    def arrivals(i, carry):
        @pl.when(i >= 1)
        def _():
            return_copy(0, i).wait_recv()

        return_copy(1, i).wait_recv()
        return carry

    return_own().wait()
    lax.fori_loop(0, R, arrivals, 0)
    rows = fin[...].reshape(R * S, Q)
    total = dot(place_v[0], rows) + dot(place_v[1], rows) + dot(place_v[2], rows)
    lout[...] = total.astype(BF16)
    stores.append(pltpu.make_async_copy(lout, layer_out, l_sem.at[3]))
    stores[3].start()

    def drain(i, carry):
        for kind in (0, 2):
            z_copy(kind, 0, i, (0, 0), (0, 1)).wait_send()

        @pl.when(i < R - 1)
        def _():
            z_copy(1, 0, i, (0, 0), (0, 1)).wait_send()
            for kind in (0, 2):
                z_copy(kind, 1, i, (0, 0), (0, 1)).wait_send()

        z_copy(1, 1, i, (0, 0), (0, 1)).wait_send()
        for kind in range(3):
            for o in range(1, J):
                exchange_copy(kind, i, o).wait_send()
        for k in range(4):
            gather(0, k, i).wait_send()
            gather(1, k, i).wait_send()
            reduce(k, i).wait_send()

        @pl.when(i >= 1)
        def _():
            return_copy(0, i).wait_send()

        return_copy(1, i).wait_send()
        return carry

    lax.fori_loop(0, R, drain, 0)
    for store in stores:
        store.wait()


def body(tokens, grad_out, expert_ids, gate_scale, gate_weight, up_weight, down_weight):
    nx = lax.axis_size("grp")
    nz = lax.axis_size("loc") // 2
    rows, Q = tokens.shape
    per_token = expert_ids.shape[1]
    F = gate_weight.shape[1]
    R, J = nz // 2, 2 * nx
    S, C = J * PAIR, J * CAP
    hbm = pl.BlockSpec(memory_space=pl.ANY)
    dma = pltpu.SemaphoreType.DMA
    outs = pl.pallas_call(
        functools.partial(layer_kernel, nx, nz),
        out_shape=(
            jax.ShapeDtypeStruct((rows, Q), BF16),
            jax.ShapeDtypeStruct((F, 4 * Q), BF16),
            jax.ShapeDtypeStruct((F, 4 * Q), BF16),
            jax.ShapeDtypeStruct((4 * F, Q), BF16),
        ),
        in_specs=[hbm] * 7,
        out_specs=(hbm,) * 4,
        scratch_shapes=[
            pltpu.VMEM((per_token, rows), jnp.int32),
            pltpu.VMEM((per_token, rows), F32),
            pltpu.VMEM((2, F, 4 * Q), BF16),
            pltpu.VMEM((4 * F, Q), BF16),
            pltpu.VMEM((R, 2, rows, Q), BF16),
            pltpu.VMEM((R, 2, rows, Q), BF16),
            pltpu.VMEM((R, 2, 2 * per_token, rows), F32),
            pltpu.VMEM((R, J, PAIR, Q), BF16),
            pltpu.VMEM((R, J, PAIR, Q), BF16),
            pltpu.VMEM((4, R, J, PAIR, Q), BF16),
            pltpu.VMEM((R, J, PAIR, Q), BF16),
            pltpu.VMEM((R, 2 * F, S), F32),
            pltpu.VMEM((4, R, F, S), BF16),
            pltpu.VMEM((R, 4, F, S), F32),
            pltpu.VMEM((R, F // 2, S), F32),
            pltpu.VMEM((R, F // 2, S), F32),
            pltpu.VMEM((R, F, S), F32),
            pltpu.VMEM((R, F, S), F32),
            pltpu.VMEM((R, J, PAIR, Q), BF16),
            pltpu.VMEM((R, J, PAIR, Q), BF16),
            pltpu.VMEM((R, 2, C, Q), BF16),
            pltpu.VMEM((R, 2, C, Q), BF16),
            pltpu.VMEM((R, 2 * F, S), BF16),
            pltpu.VMEM((2, F, 4 * Q), BF16),
            pltpu.VMEM((4 * F, Q), BF16),
            pltpu.VMEM((rows, Q), BF16),
            pltpu.VMEM((3, rows, R * S), BF16),
            dma((7,)),
            dma((2, R, 3)),
            dma((R, 2, 3)),
            dma((2, R, J)),
            dma((2, R, J)),
            dma((R, 4)),
            dma((R, 4)),
            dma((R, 4)),
            dma((R, 4)),
            dma((R, 4)),
            dma((R, 4)),
            dma((R, J)),
            dma((R, J)),
            dma((R, 2)),
            dma((R, 2)),
        ],
        compiler_params=pltpu.CompilerParams(
            collective_id=0, has_side_effects=True, vmem_limit_bytes=56 * 1024 * 1024
        ),
    )(
        expert_ids.T,
        gate_scale.T,
        tokens,
        grad_out,
        gate_weight[0],
        up_weight[0],
        down_weight[0],
    )
    return (outs[0], outs[1][None], outs[2][None], outs[3][None])


def solution(mesh):
    return jax.shard_map(
        body,
        mesh=mesh,
        in_specs=(
            P(("grp", "loc"), "dp"),
            P(("grp", "loc"), "dp"),
            P(("grp", "loc"), None),
            P(("grp", "loc"), None),
            P(("grp", "loc"), "dp", None),
            P(("grp", "loc"), "dp", None),
            P(("grp", "loc"), None, "dp"),
        ),
        out_specs=(
            P(("grp", "loc"), "dp"),
            P(("grp", "loc"), "dp", None),
            P(("grp", "loc"), "dp", None),
            P(("grp", "loc"), None, "dp"),
        ),
        check_vma=False,
    )
```

```python
import functools

import jax
import jax.numpy as jnp
from jax import lax
from jax.experimental import pallas as pl
from jax.experimental.pallas import tpu as pltpu
from jax.sharding import PartitionSpec as P

MESH = pl.DeviceIdType.MESH
CAP = 8
PAIR = 2 * CAP
BF16 = jnp.bfloat16
F32 = jnp.float32
NT = (((1,), (1,)), ((), ()))
TN = (((0,), (0,)), ((), ()))


def dot(a, b, dims=(((1,), (0,)), ((), ()))):
    return lax.dot_general(a, b, dims, preferred_element_type=F32)


def route_keys(ids, experts, planes):
    per_token, rows = ids.shape
    expert_row = lax.broadcasted_iota(jnp.int32, (experts, rows), 0)
    hits = [ids[k : k + 1, :] == expert_row for k in range(per_token)]
    named = sum(jnp.where(h, 1.0, 0.0) for h in hits).astype(BF16)
    row_at = lax.broadcasted_iota(jnp.int32, (rows, rows), 0)
    col_at = lax.broadcasted_iota(jnp.int32, (rows, rows), 1)
    before = dot(named, jnp.where(row_at < col_at, 1.0, 0.0).astype(BF16))
    ranks = jnp.concatenate(
        [jnp.sum(jnp.where(h, before, 0.0), axis=0, keepdims=True) for h in hits], axis=0
    )
    group = lax.div(ids, jnp.int32(2 * planes))
    local = ids - group * (2 * planes)
    plane = lax.div(local, jnp.int32(2))
    member = group * 2 + (local - plane * 2)
    return plane, member, ranks


def layer_kernel(
    nx, nz,
    ids_hbm, scale_hbm, tok_hbm, grad_hbm, gate_hbm, up_hbm, down_hbm,
    layer_out, gate_out, up_out, down_out,
    ids_v, scale_v, wv, dv,
    zt, zg, zm, xs, sx, slot_t,
    pre, hid, hgp, hgs, rs_half, rs_full,
    eo, rx, rz, fin, grads, place_v,
    far, l_sem, z_send, z_recv, x_send, x_recv, y_send, y_recv, s_send, s_recv, f_send, f_recv,
    far_send, far_recv,
):
    R = nz // 2
    J = 2 * nx
    per_token = ids_v.shape[0]
    Q = zt.shape[3]
    F = hid.shape[2]
    S = J * PAIR
    C = J * CAP
    y = lax.axis_index("dp")
    x = lax.axis_index("grp")
    loc = lax.axis_index("loc")
    z = loc // 2
    core = loc % 2
    me = x * 2 + core
    yp, ym, yo = (y + 1) % 4, (y + 3) % 4, (y + 2) % 4
    y_up, y_down = {"dp": yp}, {"dp": ym}

    def at_plane(p):
        return {"loc": (p % nz) * 2 + core}

    def member_at(j):
        return {"grp": j // 2, "loc": z * 2 + j % 2}

    z_right, z_left = at_plane(z + 1), at_plane(z + nz - 1)

    barrier = pltpu.get_barrier_semaphore()
    greeted = [at_plane(z + d) for d in range(1, nz)] + [y_up, y_down]
    greeted += [member_at((me + o) % J) for o in range(1, J)]
    for device in greeted:
        pl.semaphore_signal(barrier, inc=1, device_id=device, device_id_type=MESH)

    loads = [
        pltpu.make_async_copy(src, dst, l_sem.at[n])
        for n, (src, dst) in enumerate(
            [
                (ids_hbm, ids_v),
                (scale_hbm, scale_v),
                (tok_hbm, zt.at[0, 0]),
                (grad_hbm, zg.at[0, 0]),
                (gate_hbm, wv.at[0]),
                (up_hbm, wv.at[1]),
                (down_hbm, dv),
            ]
        )
    ]
    for load in loads:
        load.start()
    loads[0].wait()
    loads[1].wait()
    plane, member, ranks = route_keys(ids_v[...], nz * J, nz)
    scales = scale_v[...]
    zm[0, 0] = jnp.concatenate(
        [(plane * S + member * PAIR).astype(F32) + ranks, scales], axis=0
    )
    loads[2].wait()
    loads[3].wait()
    pl.semaphore_wait(barrier, len(greeted))

    bufs = (zt, zg, zm)

    def z_copy(kind, way, src, dst):
        return pltpu.make_async_remote_copy(
            src_ref=bufs[kind].at[src],
            dst_ref=bufs[kind].at[dst],
            send_sem=z_send.at[way, kind],
            recv_sem=z_recv.at[dst[0], dst[1], kind],
            device_id=z_right if way == 0 else z_left,
            device_id_type=MESH,
        )

    def exchange(kind):
        return ((xs, sx), (eo, rx))[kind]

    def exchange_start(kind, i):
        src, dst = exchange(kind)
        pltpu.make_async_copy(src.at[i, me], dst.at[i, me], x_recv.at[kind, i]).start()
        for o in range(1, J):
            j = (me + o) % J
            pltpu.make_async_remote_copy(
                src_ref=src.at[i, j],
                dst_ref=dst.at[i, me],
                send_sem=x_send.at[kind],
                recv_sem=x_recv.at[kind, i],
                device_id=member_at(j),
                device_id_type=MESH,
            ).start()

    def exchange_wait(kind, i):
        src, dst = exchange(kind)
        pltpu.make_async_copy(src.at[i], dst.at[i], x_recv.at[kind, i]).wait()

    def dp_copy(ref, dst, send, recv, up):
        return pltpu.make_async_remote_copy(
            src_ref=ref,
            dst_ref=dst,
            send_sem=send,
            recv_sem=recv,
            device_id=y_up if up else y_down,
            device_id_type=MESH,
        )

    def gather_buffer(kind):
        return (slot_t, hid)[kind]

    def gather(kind, k, i):
        buf = gather_buffer(kind)
        half = buf.shape[2] // 2
        lower, upper = pl.ds(0, half), pl.ds(half, half)
        ref = (buf.at[y, i], buf.at[y, i], buf.at[ym, i, lower], buf.at[yp, i, upper])[k]
        return dp_copy(ref, ref, y_send.at[kind], y_recv.at[kind, k // 2, i], k % 2 == 0)

    def reduce(k, i):
        half = F // 2
        lower, upper = pl.ds(0, half), pl.ds(half, half)
        src = (hgs.at[i, 0, lower], hgs.at[i, 0, upper], hgs.at[i, 1], hgs.at[i, 2])[k]
        dst = (rs_half, rs_full)[k // 2].at[i, k % 2]
        return dp_copy(src, dst, s_send, s_recv.at[k // 2, i], k % 2 == 0)

    def arrived(ref, sem):
        pltpu.make_async_copy(ref, ref, sem).wait()

    def return_copy(h, i):
        return pltpu.make_async_remote_copy(
            src_ref=rz.at[2 * i + h],
            dst_ref=fin.at[2 * i + h],
            send_sem=f_send,
            recv_sem=f_recv,
            device_id=at_plane(z + i) if h == 0 else at_plane(z + nz - i - 1),
            device_id_type=MESH,
        )

    def far_copy(way, leg):
        part = pl.ds(way * (C // 2), C // 2)
        last = 2 * R - 1
        return pltpu.make_async_remote_copy(
            src_ref=rz.at[last, part] if leg == 0 else far.at[way],
            dst_ref=far.at[way] if leg == 0 else fin.at[last, part],
            send_sem=f_send if leg == 0 else far_send,
            recv_sem=far_recv.at[way] if leg == 0 else f_recv,
            device_id=at_plane(z + R // 2) if way == 0 else at_plane(z + nz - R // 2),
            device_id_type=MESH,
        )

    def far_stage(i):
        for way in range(2):
            arrived(far.at[way], far_recv.at[way])
            far_copy(way, 1).start()

    def return_own():
        return pltpu.make_async_copy(rz.at[0], fin.at[0], f_recv)

    def select(i):
        marks, weights = [], 0.0
        for h in range(2):
            row_key = (
                lax.broadcasted_iota(jnp.int32, (S, zm.shape[3]), 0) + (z * S - h * CAP)
            ).astype(F32)
            table = zm[i, h]
            mark = 0.0
            for k in range(per_token):
                hit = table[k : k + 1, :] == row_key
                mark = mark + jnp.where(hit, 1.0, 0.0)
                weights = weights + jnp.where(hit, table[per_token + k : per_token + k + 1, :], 0.0)
            marks.append(mark)
        place = jnp.concatenate(marks, axis=1).astype(BF16)
        row_scale = jnp.sum(weights, axis=1, keepdims=True)
        picked_t = dot(place, zt[i].reshape(-1, Q)).astype(BF16)
        picked_g = (dot(place, zg[i].reshape(-1, Q)) * row_scale).astype(BF16)
        xs[i, :, :, 0:Q] = picked_t.reshape(J, PAIR, Q)
        xs[i, :, :, Q : 2 * Q] = picked_g.reshape(J, PAIR, Q)

    def z_stage(i):
        @pl.when(i >= 1)
        def _():
            for kind in (0, 2):
                z_copy(kind, 1, (i, 0), (i, 0)).wait_recv()

        @pl.when(i < R - 1)
        def _():
            for kind in (0, 2):
                z_copy(kind, 1, (i, 0), (i + 1, 0)).start()

        for kind in (0, 2):
            z_copy(kind, 0, (i, 1), (i, 1)).wait_recv()

        @pl.when(i < R - 1)
        def _():
            for kind in (0, 2):
                z_copy(kind, 0, (i, 1), (i + 1, 1)).start()

        @pl.when(i >= 1)
        def _():
            z_copy(1, 1, (i, 0), (i, 0)).wait_recv()

        @pl.when(i < R - 1)
        def _():
            z_copy(1, 1, (i, 0), (i + 1, 0)).start()

        @pl.when(i == R - 1)
        def _():
            z_copy(1, 1, (R - 1, 0), (R - 1, 1)).start()

        z_copy(1, 0, (i, 1), (i, 1)).wait_recv()

        @pl.when(i < R - 2)
        def _():
            z_copy(1, 0, (i, 1), (i + 1, 1)).start()

    def select_stage(i):
        select(i)
        exchange_start(0, i)

    def x_stage(i):
        exchange_wait(0, i)
        slot_t[y, i] = sx[i, :, :, 0:Q]
        gather(0, 0, i).start()
        gather(0, 1, i).start()

    def relay_stage(kind, i):
        buf = gather_buffer(kind)
        arrived(buf.at[pl.ds(0, 2), i], y_recv.at[kind, 0, i])
        gather(kind, 2, i).start()
        gather(kind, 3, i).start()

    def relay_wait(kind, i):
        arrived(gather_buffer(kind).at[yo, i], y_recv.at[kind, 1, i])

    def hidden_stage(i):
        relay_wait(0, i)
        rows = jnp.concatenate([slot_t[q, i].reshape(S, Q) for q in range(4)], axis=1)
        both = dot(wv[...].reshape(2 * F, 4 * Q), rows, NT)
        pre[i] = both
        g, u = both[0:F], both[F : 2 * F]
        hid[y, i] = (g * jax.nn.sigmoid(g) * u).astype(BF16)
        gather(1, 0, i).start()
        gather(1, 1, i).start()

    def down_stage(i):
        relay_wait(1, i)
        total = dot(hid[:, i].reshape(4 * F, S), dv[...], TN)
        eo[i] = total.astype(BF16).reshape(J, PAIR, Q)
        exchange_start(1, i)

    def return_stage(i):
        exchange_wait(1, i)
        row = lax.broadcasted_iota(jnp.int32, (S, S), 0)
        col = lax.broadcasted_iota(jnp.int32, (S, S), 1)
        h = lax.div(row, jnp.int32(C))
        j = lax.div(row - h * C, jnp.int32(CAP))
        source = j * PAIR + h * CAP + (row - h * C - j * CAP)
        swap = jnp.where(col == source, 1.0, 0.0).astype(BF16)
        rz[pl.ds(2 * i, 2)] = dot(swap, rx[i].reshape(S, Q)).astype(BF16).reshape(2, C, Q)

        @pl.when(i >= 1)
        def _():
            return_copy(0, i).start()

        @pl.when(i == 0)
        def _():
            return_own().start()

        @pl.when(i < R - 1)
        def _():
            return_copy(1, i).start()

        @pl.when(i == R - 1)
        def _():
            far_copy(0, 0).start()
            far_copy(1, 0).start()

    def sum_first(i):
        part = dot(dv[...], sx[i, :, :, Q : 2 * Q].reshape(S, Q), NT)
        hgp[i] = part.reshape(4, F, S)
        hgs[i, 0] = hgp[i, yo].astype(BF16)
        reduce(0, i).start()
        reduce(1, i).start()

    def sum_second(i):
        half = F // 2
        arrived(rs_half.at[i], s_recv.at[0, i])
        hgs[i, 1, 0:half] = (hgp[i, yp, 0:half] + rs_half[i, 0].astype(F32)).astype(BF16)
        hgs[i, 1, half:F] = hgp[i, yp, half:F].astype(BF16)
        reduce(2, i).start()
        hgs[i, 2, half:F] = (hgp[i, ym, half:F] + rs_half[i, 1].astype(F32)).astype(BF16)
        hgs[i, 2, 0:half] = hgp[i, ym, 0:half].astype(BF16)
        reduce(3, i).start()

    def sum_last(i):
        arrived(rs_full.at[i], s_recv.at[1, i])
        hidden_grad = hgp[i, y] + rs_full[i, 0].astype(F32) + rs_full[i, 1].astype(F32)
        g, u = pre[i, 0:F], pre[i, F : 2 * F]
        s = jax.nn.sigmoid(g)
        gate_grad = hidden_grad * u * s * (1.0 + g * (1.0 - s))
        up_grad = hidden_grad * (g * s)
        grads[i] = jnp.concatenate([gate_grad, up_grad], axis=0).astype(BF16)

    for kind in (0, 2, 1):
        z_copy(kind, 0, (0, 0), (0, 1)).start()

    delta = z - plane
    delta = jnp.where(delta < 0, delta + nz, delta)
    back = jnp.where(delta < R, delta * 2, (nz - 1 - delta) * 2 + 1)
    row_of = (back * C + member * CAP).astype(F32) + ranks
    packed = jnp.concatenate([row_of, scales], axis=0)
    tokens = packed.shape[1]
    packed = jnp.concatenate(
        [packed, jnp.zeros((tokens - 2 * per_token, tokens), F32)], axis=0
    ).T
    for r in range(R):
        lane = (lax.broadcasted_iota(jnp.int32, (tokens, 2 * C), 1) + r * 2 * C).astype(F32)
        weight = 0.0
        for k in range(per_token):
            hit = packed[:, k : k + 1] == lane
            weight = weight + jnp.where(hit, packed[:, per_token + k : per_token + k + 1], 0.0)
        for part in range(3):
            piece = weight.astype(BF16)
            place_v[part, :, r * 2 * C : (r + 1) * 2 * C] = piece
            weight = weight - piece.astype(F32)
    for load in loads[4:]:
        load.wait()

    stages = (
        (0, z_stage),
        (6, return_stage),
        (5, down_stage),
        (4, functools.partial(relay_stage, 1)),
        (3, hidden_stage),
        (2, functools.partial(relay_stage, 0)),
        (1, x_stage),
        (0, select_stage),
    )
    sums = ((10, sum_last), (9, sum_second), (8, sum_first))

    def step(i, carry):
        for lag, stage in stages:

            @pl.when((i >= lag) & (i < R + lag))
            def _(lag=lag, stage=stage):
                stage(i - lag)

        @pl.when(i == R + 6)
        def _():
            far_stage(i)

        for lag, stage in sums:

            @pl.when((i >= lag) & (i < R // 2 + lag))
            def _(lag=lag, stage=stage):
                stage((i - lag) * 2)
                stage((i - lag) * 2 + 1)

        return carry

    lax.fori_loop(0, R + 7, step, 0)

    flat_g = sx[:, :, :, Q : 2 * Q].reshape(R * S, Q)
    for q in range(4):
        lhs = jnp.concatenate([hid[q, r] for r in range(R)], axis=1)
        down_out[q * F : (q + 1) * F] = dot(lhs, flat_g).astype(BF16)
    lhs = jnp.concatenate([grads[r] for r in range(R)], axis=1)
    for q in range(4):
        res = dot(lhs, slot_t[q].reshape(R * S, Q)).astype(BF16)
        gate_out[:, q * Q : (q + 1) * Q] = res[0:F]
        up_out[:, q * Q : (q + 1) * Q] = res[F : 2 * F]

    arrived(zt.at[:, 0], z_send.at[0, 0])
    arrived(zm.at[:, 0], z_send.at[0, 2])
    arrived(zg.at[pl.ds(0, R - 1), 0], z_send.at[0, 1])
    arrived(zt.at[pl.ds(0, R - 1), 0], z_send.at[1, 0])
    arrived(zm.at[pl.ds(0, R - 1), 0], z_send.at[1, 2])
    arrived(zg.at[:, 0], z_send.at[1, 1])
    arrived(xs.at[:, pl.ds(0, J - 1)], x_send.at[0])
    arrived(eo.at[:, pl.ds(0, J - 1)], x_send.at[1])
    arrived(slot_t.at[pl.ds(0, 3)], y_send.at[0])
    arrived(hid.at[pl.ds(0, 3)], y_send.at[1])
    arrived(hgs, s_send)
    arrived(fin, f_recv)
    rows = fin[...].reshape(R * S, Q)
    total = dot(place_v[0], rows) + dot(place_v[1], rows) + dot(place_v[2], rows)
    layer_out[...] = total.astype(BF16)
    arrived(rz.at[pl.ds(0, 2 * R - 1)], f_send)
    arrived(far, far_send)


def body(tokens, grad_out, expert_ids, gate_scale, gate_weight, up_weight, down_weight):
    nx = lax.axis_size("grp")
    nz = lax.axis_size("loc") // 2
    rows, Q = tokens.shape
    per_token = expert_ids.shape[1]
    F = gate_weight.shape[1]
    R, J = nz // 2, 2 * nx
    S, C = J * PAIR, J * CAP
    hbm = pl.BlockSpec(memory_space=pltpu.HBM)
    dma = pltpu.SemaphoreType.DMA
    outs = pl.pallas_call(
        functools.partial(layer_kernel, nx, nz),
        out_shape=(
            jax.ShapeDtypeStruct((rows, Q), BF16),
            jax.ShapeDtypeStruct((F, 4 * Q), BF16),
            jax.ShapeDtypeStruct((F, 4 * Q), BF16),
            jax.ShapeDtypeStruct((4 * F, Q), BF16),
        ),
        in_specs=[hbm] * 7,
        out_specs=(pl.BlockSpec(memory_space=pltpu.VMEM),) * 4,
        scratch_shapes=[
            pltpu.VMEM((per_token, rows), jnp.int32),
            pltpu.VMEM((per_token, rows), F32),
            pltpu.VMEM((2, F, 4 * Q), BF16),
            pltpu.VMEM((4 * F, Q), BF16),
            pltpu.VMEM((R, 2, rows, Q), BF16),
            pltpu.VMEM((R, 2, rows, Q), BF16),
            pltpu.VMEM((R, 2, 2 * per_token, rows), F32),
            pltpu.VMEM((R, J, PAIR, 2 * Q), BF16),
            pltpu.VMEM((R, J, PAIR, 2 * Q), BF16),
            pltpu.VMEM((4, R, J, PAIR, Q), BF16),
            pltpu.VMEM((R, 2 * F, S), F32),
            pltpu.VMEM((4, R, F, S), BF16),
            pltpu.VMEM((R, 4, F, S), F32),
            pltpu.VMEM((R, 3, F, S), BF16),
            pltpu.VMEM((R, 2, F // 2, S), BF16),
            pltpu.VMEM((R, 2, F, S), BF16),
            pltpu.VMEM((R, J, PAIR, Q), BF16),
            pltpu.VMEM((R, J, PAIR, Q), BF16),
            pltpu.VMEM((2 * R, C, Q), BF16),
            pltpu.VMEM((2 * R, C, Q), BF16),
            pltpu.VMEM((R, 2 * F, S), BF16),
            pltpu.VMEM((3, rows, R * S), BF16),
            pltpu.VMEM((2, C // 2, Q), BF16),
            dma((7,)),
            dma((2, 3)),
            dma((R, 2, 3)),
            dma((2,)),
            dma((2, R)),
            dma((2,)),
            dma((2, 2, R)),
            dma(()),
            dma((2, R)),
            dma(()),
            dma(()),
            dma(()),
            dma((2,)),
        ],
        compiler_params=pltpu.CompilerParams(
            collective_id=0, has_side_effects=True, vmem_limit_bytes=48 * 1024 * 1024
        ),
    )(
        *(
            pltpu.with_memory_space_constraint(a, pltpu.HBM)
            for a in (
                expert_ids.T,
                gate_scale.T,
                tokens,
                grad_out,
                gate_weight[0],
                up_weight[0],
                down_weight[0],
            )
        )
    )
    return (outs[0], outs[1][None], outs[2][None], outs[3][None])


def solution(mesh):
    return jax.shard_map(
        body,
        mesh=mesh,
        in_specs=(
            P(("grp", "loc"), "dp"),
            P(("grp", "loc"), "dp"),
            P(("grp", "loc"), None),
            P(("grp", "loc"), None),
            P(("grp", "loc"), "dp", None),
            P(("grp", "loc"), "dp", None),
            P(("grp", "loc"), None, "dp"),
        ),
        out_specs=(
            P(("grp", "loc"), "dp"),
            P(("grp", "loc"), "dp", None),
            P(("grp", "loc"), "dp", None),
            P(("grp", "loc"), None, "dp"),
        ),
        check_vma=False,
    )
```

```python
import functools

import jax
import jax.numpy as jnp
from jax import lax
from jax.experimental import pallas as pl
from jax.experimental.pallas import tpu as pltpu
from jax.sharding import PartitionSpec as P

MESH = pl.DeviceIdType.MESH
CAP = 8
PAIR = 2 * CAP
BF16 = jnp.bfloat16
F32 = jnp.float32
NT = (((1,), (1,)), ((), ()))
TN = (((0,), (0,)), ((), ()))


def dot(a, b, dims=(((1,), (0,)), ((), ()))):
    return lax.dot_general(a, b, dims, preferred_element_type=F32)


def route_keys(ids, experts, planes):
    per_token, rows = ids.shape
    expert_row = lax.broadcasted_iota(jnp.int32, (experts, rows), 0)
    hits = [ids[k : k + 1, :] == expert_row for k in range(per_token)]
    named = sum(jnp.where(h, 1.0, 0.0) for h in hits).astype(BF16)
    row_at = lax.broadcasted_iota(jnp.int32, (rows, rows), 0)
    col_at = lax.broadcasted_iota(jnp.int32, (rows, rows), 1)
    before = dot(named, jnp.where(row_at < col_at, 1.0, 0.0).astype(BF16))
    ranks = jnp.concatenate(
        [jnp.sum(jnp.where(h, before, 0.0), axis=0, keepdims=True) for h in hits], axis=0
    )
    group = lax.div(ids, jnp.int32(2 * planes))
    local = ids - group * (2 * planes)
    plane = lax.div(local, jnp.int32(2))
    member = group * 2 + (local - plane * 2)
    return plane, member, ranks


def layer_kernel(
    nx, nz,
    ids_hbm, scale_hbm, tok_hbm, grad_hbm, gate_hbm, up_hbm, down_hbm,
    layer_out, gate_out, up_out, down_out,
    ids_v, scale_v, wv, dv,
    zt, zg, zm, xs, sx, slot_t,
    pre, hid, hgp, hgs, rs_half, rs_full,
    eo, rx, rz, fin, grads, place_v,
    l_sem, z_send, z_recv, x_send, x_recv, y_send, y_recv, s_send, s_recv, f_send, f_recv,
):
    R = nz // 2
    J = 2 * nx
    per_token = ids_v.shape[0]
    Q = zt.shape[3]
    F = hid.shape[2]
    S = J * PAIR
    C = J * CAP
    y = lax.axis_index("dp")
    x = lax.axis_index("grp")
    loc = lax.axis_index("loc")
    z = loc // 2
    core = loc % 2
    me = x * 2 + core
    yp, ym, yo = (y + 1) % 4, (y + 3) % 4, (y + 2) % 4
    y_up, y_down = {"dp": yp}, {"dp": ym}

    def at_plane(p):
        return {"loc": (p % nz) * 2 + core}

    def member_at(j):
        return {"grp": j // 2, "loc": z * 2 + j % 2}

    z_right, z_left = at_plane(z + 1), at_plane(z + nz - 1)

    barrier = pltpu.get_barrier_semaphore()
    greeted = [at_plane(z + d) for d in range(1, nz)] + [y_up, y_down]
    greeted += [member_at((me + o) % J) for o in range(1, J)]
    for device in greeted:
        pl.semaphore_signal(barrier, inc=1, device_id=device, device_id_type=MESH)

    loads = [
        pltpu.make_async_copy(src, dst, l_sem.at[n])
        for n, (src, dst) in enumerate(
            [
                (ids_hbm, ids_v),
                (scale_hbm, scale_v),
                (tok_hbm, zt.at[0, 0]),
                (grad_hbm, zg.at[0, 0]),
                (gate_hbm, wv.at[0]),
                (up_hbm, wv.at[1]),
                (down_hbm, dv),
            ]
        )
    ]
    for load in loads:
        load.start()
    loads[0].wait()
    loads[1].wait()
    plane, member, ranks = route_keys(ids_v[...], nz * J, nz)
    scales = scale_v[...]
    zm[0, 0] = jnp.concatenate(
        [(plane * S + member * PAIR).astype(F32) + ranks, scales], axis=0
    )
    loads[2].wait()
    loads[3].wait()
    pl.semaphore_wait(barrier, len(greeted))

    bufs = (zt, zg, zm)

    def z_copy(kind, way, src, dst):
        return pltpu.make_async_remote_copy(
            src_ref=bufs[kind].at[src],
            dst_ref=bufs[kind].at[dst],
            send_sem=z_send.at[way, kind],
            recv_sem=z_recv.at[dst[0], dst[1], kind],
            device_id=z_right if way == 0 else z_left,
            device_id_type=MESH,
        )

    def exchange(kind):
        return ((xs, sx), (eo, rx))[kind]

    def exchange_start(kind, i):
        src, dst = exchange(kind)
        pltpu.make_async_copy(src.at[i, me], dst.at[i, me], x_recv.at[kind, i]).start()
        for o in range(1, J):
            j = (me + o) % J
            pltpu.make_async_remote_copy(
                src_ref=src.at[i, j],
                dst_ref=dst.at[i, me],
                send_sem=x_send.at[kind],
                recv_sem=x_recv.at[kind, i],
                device_id=member_at(j),
                device_id_type=MESH,
            ).start()

    def exchange_wait(kind, i):
        src, dst = exchange(kind)
        pltpu.make_async_copy(src.at[i], dst.at[i], x_recv.at[kind, i]).wait()

    def dp_copy(ref, dst, send, recv, up):
        return pltpu.make_async_remote_copy(
            src_ref=ref,
            dst_ref=dst,
            send_sem=send,
            recv_sem=recv,
            device_id=y_up if up else y_down,
            device_id_type=MESH,
        )

    def gather_buffer(kind):
        return (slot_t, hid)[kind]

    def gather(kind, k, i):
        buf = gather_buffer(kind)
        half = buf.shape[2] // 2
        lower, upper = pl.ds(0, half), pl.ds(half, half)
        ref = (buf.at[y, i], buf.at[y, i], buf.at[ym, i, lower], buf.at[yp, i, upper])[k]
        return dp_copy(ref, ref, y_send.at[kind], y_recv.at[kind, k // 2, i], k % 2 == 0)

    def reduce(k, i):
        half = F // 2
        lower, upper = pl.ds(0, half), pl.ds(half, half)
        src = (hgs.at[i, 0, lower], hgs.at[i, 0, upper], hgs.at[i, 1], hgs.at[i, 2])[k]
        dst = (rs_half, rs_full)[k // 2].at[i, k % 2]
        return dp_copy(src, dst, s_send, s_recv.at[k // 2, i], k % 2 == 0)

    def arrived(ref, sem):
        pltpu.make_async_copy(ref, ref, sem).wait()

    def return_copy(h, i):
        return pltpu.make_async_remote_copy(
            src_ref=rz.at[2 * i + h],
            dst_ref=fin.at[2 * i + h],
            send_sem=f_send,
            recv_sem=f_recv,
            device_id=at_plane(z + i) if h == 0 else at_plane(z + nz - i - 1),
            device_id_type=MESH,
        )

    def return_own():
        return pltpu.make_async_copy(rz.at[0], fin.at[0], f_recv)

    def select(i):
        marks, weights = [], 0.0
        for h in range(2):
            row_key = (
                lax.broadcasted_iota(jnp.int32, (S, zm.shape[3]), 0) + (z * S - h * CAP)
            ).astype(F32)
            table = zm[i, h]
            mark = 0.0
            for k in range(per_token):
                hit = table[k : k + 1, :] == row_key
                mark = mark + jnp.where(hit, 1.0, 0.0)
                weights = weights + jnp.where(hit, table[per_token + k : per_token + k + 1, :], 0.0)
            marks.append(mark)
        place = jnp.concatenate(marks, axis=1).astype(BF16)
        row_scale = jnp.sum(weights, axis=1, keepdims=True)
        picked_t = dot(place, zt[i].reshape(-1, Q)).astype(BF16)
        picked_g = (dot(place, zg[i].reshape(-1, Q)) * row_scale).astype(BF16)
        xs[i, :, :, 0:Q] = picked_t.reshape(J, PAIR, Q)
        xs[i, :, :, Q : 2 * Q] = picked_g.reshape(J, PAIR, Q)

    def z_stage(i):
        @pl.when(i >= 1)
        def _():
            for kind in (0, 2):
                z_copy(kind, 1, (i, 0), (i, 0)).wait_recv()

        @pl.when(i < R - 1)
        def _():
            for kind in (0, 2):
                z_copy(kind, 1, (i, 0), (i + 1, 0)).start()

        for kind in (0, 2):
            z_copy(kind, 0, (i, 1), (i, 1)).wait_recv()

        @pl.when(i < R - 1)
        def _():
            for kind in (0, 2):
                z_copy(kind, 0, (i, 1), (i + 1, 1)).start()

        @pl.when(i >= 1)
        def _():
            z_copy(1, 1, (i, 0), (i, 0)).wait_recv()

        @pl.when(i < R - 1)
        def _():
            z_copy(1, 1, (i, 0), (i + 1, 0)).start()

        @pl.when(i == R - 1)
        def _():
            z_copy(1, 1, (R - 1, 0), (R - 1, 1)).start()

        z_copy(1, 0, (i, 1), (i, 1)).wait_recv()

        @pl.when(i < R - 2)
        def _():
            z_copy(1, 0, (i, 1), (i + 1, 1)).start()

    def select_stage(i):
        select(i)
        exchange_start(0, i)

    def x_stage(i):
        exchange_wait(0, i)
        slot_t[y, i] = sx[i, :, :, 0:Q]
        gather(0, 0, i).start()
        gather(0, 1, i).start()

    def relay_stage(kind, i):
        buf = gather_buffer(kind)
        arrived(buf.at[pl.ds(0, 2), i], y_recv.at[kind, 0, i])
        gather(kind, 2, i).start()
        gather(kind, 3, i).start()

    def relay_wait(kind, i):
        arrived(gather_buffer(kind).at[yo, i], y_recv.at[kind, 1, i])

    def hidden_stage(i):
        relay_wait(0, i)
        rows = jnp.concatenate([slot_t[q, i].reshape(S, Q) for q in range(4)], axis=1)
        both = dot(wv[...].reshape(2 * F, 4 * Q), rows, NT)
        pre[i] = both
        g, u = both[0:F], both[F : 2 * F]
        hid[y, i] = (g * jax.nn.sigmoid(g) * u).astype(BF16)
        gather(1, 0, i).start()
        gather(1, 1, i).start()

    def down_stage(i):
        relay_wait(1, i)
        total = dot(hid[:, i].reshape(4 * F, S), dv[...], TN)
        eo[i] = total.astype(BF16).reshape(J, PAIR, Q)
        exchange_start(1, i)

    def return_stage(i):
        exchange_wait(1, i)
        row = lax.broadcasted_iota(jnp.int32, (S, S), 0)
        col = lax.broadcasted_iota(jnp.int32, (S, S), 1)
        h = lax.div(row, jnp.int32(C))
        j = lax.div(row - h * C, jnp.int32(CAP))
        source = j * PAIR + h * CAP + (row - h * C - j * CAP)
        swap = jnp.where(col == source, 1.0, 0.0).astype(BF16)
        rz[pl.ds(2 * i, 2)] = dot(swap, rx[i].reshape(S, Q)).astype(BF16).reshape(2, C, Q)

        @pl.when(i >= 1)
        def _():
            return_copy(0, i).start()

        @pl.when(i == 0)
        def _():
            return_own().start()

        return_copy(1, i).start()

    def sum_part(i):
        part = dot(dv[...], sx[i, :, :, Q : 2 * Q].reshape(S, Q), NT)
        hgp[i] = part.reshape(4, F, S)
        hgs[i, 0] = hgp[i, yo].astype(BF16)

    def sum_first(i):
        reduce(0, i).start()
        reduce(1, i).start()

    def sum_second(i):
        half = F // 2
        arrived(rs_half.at[i], s_recv.at[0, i])
        hgs[i, 1, 0:half] = (hgp[i, yp, 0:half] + rs_half[i, 0].astype(F32)).astype(BF16)
        hgs[i, 1, half:F] = hgp[i, yp, half:F].astype(BF16)
        reduce(2, i).start()
        hgs[i, 2, half:F] = (hgp[i, ym, half:F] + rs_half[i, 1].astype(F32)).astype(BF16)
        hgs[i, 2, 0:half] = hgp[i, ym, 0:half].astype(BF16)
        reduce(3, i).start()

    def sum_last(i):
        arrived(rs_full.at[i], s_recv.at[1, i])
        hidden_grad = hgp[i, y] + rs_full[i, 0].astype(F32) + rs_full[i, 1].astype(F32)
        g, u = pre[i, 0:F], pre[i, F : 2 * F]
        s = jax.nn.sigmoid(g)
        gate_grad = hidden_grad * u * s * (1.0 + g * (1.0 - s))
        up_grad = hidden_grad * (g * s)
        grads[i] = jnp.concatenate([gate_grad, up_grad], axis=0).astype(BF16)

    for kind in (0, 2, 1):
        z_copy(kind, 0, (0, 0), (0, 1)).start()

    delta = z - plane
    delta = jnp.where(delta < 0, delta + nz, delta)
    back = jnp.where(delta < R, delta * 2, (nz - 1 - delta) * 2 + 1)
    row_of = (back * C + member * CAP).astype(F32) + ranks
    packed = jnp.concatenate([row_of, scales], axis=0)
    tokens = packed.shape[1]
    packed = jnp.concatenate(
        [packed, jnp.zeros((tokens - 2 * per_token, tokens), F32)], axis=0
    ).T
    for r in range(R):
        lane = (lax.broadcasted_iota(jnp.int32, (tokens, 2 * C), 1) + r * 2 * C).astype(F32)
        weight = 0.0
        for k in range(per_token):
            hit = packed[:, k : k + 1] == lane
            weight = weight + jnp.where(hit, packed[:, per_token + k : per_token + k + 1], 0.0)
        for part in range(3):
            piece = weight.astype(BF16)
            place_v[part, :, r * 2 * C : (r + 1) * 2 * C] = piece
            weight = weight - piece.astype(F32)
    for load in loads[4:]:
        load.wait()

    stages = (
        (0, z_stage),
        (6, return_stage),
        (5, down_stage),
        (4, functools.partial(relay_stage, 1)),
        (3, hidden_stage),
        (2, functools.partial(relay_stage, 0)),
        (1, x_stage),
        (0, select_stage),
        (2, sum_part),
    )
    sums = ((10, sum_last), (9, sum_second), (8, sum_first))

    def step(i, carry):
        for lag, stage in stages:

            @pl.when((i >= lag) & (i < R + lag))
            def _(lag=lag, stage=stage):
                stage(i - lag)

        for lag, stage in sums:

            @pl.when((i >= lag) & (i < R // 2 + lag))
            def _(lag=lag, stage=stage):
                stage((i - lag) * 2)
                stage((i - lag) * 2 + 1)

        return carry

    lax.fori_loop(0, R + 6, step, 0)

    flat_g = sx[:, :, :, Q : 2 * Q].reshape(R * S, Q)
    for q in range(4):
        lhs = jnp.concatenate([hid[q, r] for r in range(R)], axis=1)
        down_out[q * F : (q + 1) * F] = dot(lhs, flat_g).astype(BF16)
    lhs = jnp.concatenate([grads[r] for r in range(R)], axis=1)
    for q in range(4):
        res = dot(lhs, slot_t[q].reshape(R * S, Q)).astype(BF16)
        gate_out[:, q * Q : (q + 1) * Q] = res[0:F]
        up_out[:, q * Q : (q + 1) * Q] = res[F : 2 * F]

    arrived(zt.at[:, 0], z_send.at[0, 0])
    arrived(zm.at[:, 0], z_send.at[0, 2])
    arrived(zg.at[pl.ds(0, R - 1), 0], z_send.at[0, 1])
    arrived(zt.at[pl.ds(0, R - 1), 0], z_send.at[1, 0])
    arrived(zm.at[pl.ds(0, R - 1), 0], z_send.at[1, 2])
    arrived(zg.at[:, 0], z_send.at[1, 1])
    arrived(xs.at[:, pl.ds(0, J - 1)], x_send.at[0])
    arrived(eo.at[:, pl.ds(0, J - 1)], x_send.at[1])
    arrived(slot_t.at[pl.ds(0, 3)], y_send.at[0])
    arrived(hid.at[pl.ds(0, 3)], y_send.at[1])
    arrived(hgs, s_send)
    arrived(fin, f_recv)
    rows = fin[...].reshape(R * S, Q)
    total = dot(place_v[0], rows) + dot(place_v[1], rows) + dot(place_v[2], rows)
    layer_out[...] = total.astype(BF16)
    arrived(rz.at[pl.ds(0, 2 * R - 1)], f_send)


def store_kernel(*refs):
    sems = refs[8]
    copies = [pltpu.make_async_copy(refs[n], refs[4 + n], sems.at[n]) for n in range(4)]
    for copy in copies:
        copy.start()
    for copy in copies:
        copy.wait()


def body(tokens, grad_out, expert_ids, gate_scale, gate_weight, up_weight, down_weight):
    nx = lax.axis_size("grp")
    nz = lax.axis_size("loc") // 2
    rows, Q = tokens.shape
    per_token = expert_ids.shape[1]
    F = gate_weight.shape[1]
    R, J = nz // 2, 2 * nx
    S, C = J * PAIR, J * CAP
    hbm = pl.BlockSpec(memory_space=pltpu.HBM)
    dma = pltpu.SemaphoreType.DMA
    outs = pl.pallas_call(
        functools.partial(layer_kernel, nx, nz),
        out_shape=(
            jax.ShapeDtypeStruct((rows, Q), BF16),
            jax.ShapeDtypeStruct((F, 4 * Q), BF16),
            jax.ShapeDtypeStruct((F, 4 * Q), BF16),
            jax.ShapeDtypeStruct((4 * F, Q), BF16),
        ),
        in_specs=[hbm] * 7,
        out_specs=(pl.BlockSpec(memory_space=pltpu.VMEM),) * 4,
        scratch_shapes=[
            pltpu.VMEM((per_token, rows), jnp.int32),
            pltpu.VMEM((per_token, rows), F32),
            pltpu.VMEM((2, F, 4 * Q), BF16),
            pltpu.VMEM((4 * F, Q), BF16),
            pltpu.VMEM((R, 2, rows, Q), BF16),
            pltpu.VMEM((R, 2, rows, Q), BF16),
            pltpu.VMEM((R, 2, 2 * per_token, rows), F32),
            pltpu.VMEM((R, J, PAIR, 2 * Q), BF16),
            pltpu.VMEM((R, J, PAIR, 2 * Q), BF16),
            pltpu.VMEM((4, R, J, PAIR, Q), BF16),
            pltpu.VMEM((R, 2 * F, S), F32),
            pltpu.VMEM((4, R, F, S), BF16),
            pltpu.VMEM((R, 4, F, S), F32),
            pltpu.VMEM((R, 3, F, S), BF16),
            pltpu.VMEM((R, 2, F // 2, S), BF16),
            pltpu.VMEM((R, 2, F, S), BF16),
            pltpu.VMEM((R, J, PAIR, Q), BF16),
            pltpu.VMEM((R, J, PAIR, Q), BF16),
            pltpu.VMEM((2 * R, C, Q), BF16),
            pltpu.VMEM((2 * R, C, Q), BF16),
            pltpu.VMEM((R, 2 * F, S), BF16),
            pltpu.VMEM((3, rows, R * S), BF16),
            dma((7,)),
            dma((2, 3)),
            dma((R, 2, 3)),
            dma((2,)),
            dma((2, R)),
            dma((2,)),
            dma((2, 2, R)),
            dma(()),
            dma((2, R)),
            dma(()),
            dma(()),
        ],
        compiler_params=pltpu.CompilerParams(
            collective_id=0, has_side_effects=True, vmem_limit_bytes=48 * 1024 * 1024
        ),
    )(
        *(
            pltpu.with_memory_space_constraint(a, pltpu.HBM)
            for a in (
                expert_ids.T,
                gate_scale.T,
                tokens,
                grad_out,
                gate_weight[0],
                up_weight[0],
                down_weight[0],
            )
        )
    )
    outs = pl.pallas_call(
        store_kernel,
        out_shape=tuple(jax.ShapeDtypeStruct(o.shape, o.dtype) for o in outs),
        in_specs=[pl.BlockSpec(memory_space=pltpu.VMEM)] * 4,
        out_specs=(hbm,) * 4,
        scratch_shapes=[dma((4,))],
        compiler_params=pltpu.CompilerParams(vmem_limit_bytes=8 * 1024 * 1024),
    )(*outs)
    return (outs[0], outs[1][None], outs[2][None], outs[3][None])


def solution(mesh):
    return jax.shard_map(
        body,
        mesh=mesh,
        in_specs=(
            P(("grp", "loc"), "dp"),
            P(("grp", "loc"), "dp"),
            P(("grp", "loc"), None),
            P(("grp", "loc"), None),
            P(("grp", "loc"), "dp", None),
            P(("grp", "loc"), "dp", None),
            P(("grp", "loc"), None, "dp"),
        ),
        out_specs=(
            P(("grp", "loc"), "dp"),
            P(("grp", "loc"), "dp", None),
            P(("grp", "loc"), "dp", None),
            P(("grp", "loc"), None, "dp"),
        ),
        check_vma=False,
    )
```

```python
import functools

import jax
import jax.numpy as jnp
from jax import lax
from jax.experimental import pallas as pl
from jax.experimental.pallas import tpu as pltpu
from jax.sharding import PartitionSpec as P

MESH = pl.DeviceIdType.MESH
CAP = 8
PAIR = 2 * CAP
BF16 = jnp.bfloat16
F32 = jnp.float32
NT = (((1,), (1,)), ((), ()))
TN = (((0,), (0,)), ((), ()))


def dot(a, b, dims=(((1,), (0,)), ((), ()))):
    return lax.dot_general(a, b, dims, preferred_element_type=F32)


def route_keys(ids, experts, planes):
    per_token, rows = ids.shape
    expert_row = lax.broadcasted_iota(jnp.int32, (experts, rows), 0)
    hits = [ids[k : k + 1, :] == expert_row for k in range(per_token)]
    named = sum(jnp.where(h, 1.0, 0.0) for h in hits).astype(BF16)
    row_at = lax.broadcasted_iota(jnp.int32, (rows, rows), 0)
    col_at = lax.broadcasted_iota(jnp.int32, (rows, rows), 1)
    before = dot(named, jnp.where(row_at < col_at, 1.0, 0.0).astype(BF16))
    ranks = jnp.concatenate(
        [jnp.sum(jnp.where(h, before, 0.0), axis=0, keepdims=True) for h in hits], axis=0
    )
    group = lax.div(ids, jnp.int32(2 * planes))
    local = ids - group * (2 * planes)
    plane = lax.div(local, jnp.int32(2))
    member = group * 2 + (local - plane * 2)
    return plane, member, ranks


def layer_kernel(
    nx, nz,
    ids_hbm, scale_hbm, tok_hbm, grad_hbm, gate_hbm, up_hbm, down_hbm,
    layer_out, gate_out, up_out, down_out,
    ids_v, scale_v, wv, dv,
    zt, zg, zm, xs, sx, slot_t,
    pre, hid, hgp, hgs, rs_half, rs_full,
    eo, rx, rz, fin, grads, place_v,
    l_sem, z_send, z_recv, x_send, x_recv, y_send, y_recv, s_send, s_recv, f_send, f_recv,
):
    R = nz // 2
    J = 2 * nx
    per_token = ids_v.shape[0]
    Q = zt.shape[3]
    F = hid.shape[2]
    S = J * PAIR
    C = J * CAP
    y = lax.axis_index("dp")
    x = lax.axis_index("grp")
    loc = lax.axis_index("loc")
    z = loc // 2
    core = loc % 2
    me = x * 2 + core
    yp, ym, yo = (y + 1) % 4, (y + 3) % 4, (y + 2) % 4
    y_up, y_down = {"dp": yp}, {"dp": ym}

    def at_plane(p):
        return {"loc": (p % nz) * 2 + core}

    def member_at(j):
        return {"grp": j // 2, "loc": z * 2 + j % 2}

    z_right, z_left = at_plane(z + 1), at_plane(z + nz - 1)

    barrier = pltpu.get_barrier_semaphore()
    greeted = [at_plane(z + d) for d in range(1, nz)] + [y_up, y_down]
    greeted += [member_at((me + o) % J) for o in range(1, J)]
    for device in greeted:
        pl.semaphore_signal(barrier, inc=1, device_id=device, device_id_type=MESH)

    loads = [
        pltpu.make_async_copy(src, dst, l_sem.at[n])
        for n, (src, dst) in enumerate(
            [
                (ids_hbm, ids_v),
                (scale_hbm, scale_v),
                (tok_hbm, zt.at[0, 0]),
                (grad_hbm, zg.at[0, 0]),
                (gate_hbm, wv.at[0]),
                (up_hbm, wv.at[1]),
                (down_hbm, dv),
            ]
        )
    ]
    for load in loads:
        load.start()
    loads[0].wait()
    loads[1].wait()
    plane, member, ranks = route_keys(ids_v[...], nz * J, nz)
    scales = scale_v[...]
    zm[0, 0] = jnp.concatenate(
        [(plane * S + member * PAIR).astype(F32) + ranks, scales], axis=0
    )
    loads[2].wait()
    loads[3].wait()
    pl.semaphore_wait(barrier, len(greeted))

    bufs = (zt, zg, zm)

    def z_copy(kind, way, src, dst):
        return pltpu.make_async_remote_copy(
            src_ref=bufs[kind].at[src],
            dst_ref=bufs[kind].at[dst],
            send_sem=z_send.at[way, kind],
            recv_sem=z_recv.at[dst[0], dst[1], kind],
            device_id=z_right if way == 0 else z_left,
            device_id_type=MESH,
        )

    def exchange(kind):
        return ((xs, sx), (eo, rx))[kind]

    def exchange_start(kind, i):
        src, dst = exchange(kind)
        pltpu.make_async_copy(src.at[i, me], dst.at[i, me], x_recv.at[kind, i]).start()
        for o in range(1, J):
            j = (me + o) % J
            pltpu.make_async_remote_copy(
                src_ref=src.at[i, j],
                dst_ref=dst.at[i, me],
                send_sem=x_send.at[kind],
                recv_sem=x_recv.at[kind, i],
                device_id=member_at(j),
                device_id_type=MESH,
            ).start()

    def exchange_wait(kind, i):
        src, dst = exchange(kind)
        pltpu.make_async_copy(src.at[i], dst.at[i], x_recv.at[kind, i]).wait()

    def dp_copy(ref, dst, send, recv, up):
        return pltpu.make_async_remote_copy(
            src_ref=ref,
            dst_ref=dst,
            send_sem=send,
            recv_sem=recv,
            device_id=y_up if up else y_down,
            device_id_type=MESH,
        )

    def gather_buffer(kind):
        return (slot_t, hid)[kind]

    def gather(kind, k, i):
        buf = gather_buffer(kind)
        half = buf.shape[2] // 2
        lower, upper = pl.ds(0, half), pl.ds(half, half)
        ref = (buf.at[y, i], buf.at[y, i], buf.at[ym, i, lower], buf.at[yp, i, upper])[k]
        return dp_copy(ref, ref, y_send.at[kind], y_recv.at[kind, k // 2, i], k % 2 == 0)

    def reduce(k, i):
        half = F // 2
        lower, upper = pl.ds(0, half), pl.ds(half, half)
        src = (hgs.at[i, 0, lower], hgs.at[i, 0, upper], hgs.at[i, 1], hgs.at[i, 2])[k]
        dst = (rs_half, rs_full)[k // 2].at[i, k % 2]
        return dp_copy(src, dst, s_send, s_recv.at[k // 2, i], k % 2 == 0)

    def arrived(ref, sem):
        pltpu.make_async_copy(ref, ref, sem).wait()

    def return_copy(h, i):
        return pltpu.make_async_remote_copy(
            src_ref=rz.at[2 * i + h],
            dst_ref=fin.at[2 * i + h],
            send_sem=f_send,
            recv_sem=f_recv.at[i // (R - 2)],
            device_id=at_plane(z + i) if h == 0 else at_plane(z + nz - i - 1),
            device_id_type=MESH,
        )

    def return_own():
        return pltpu.make_async_copy(rz.at[0], fin.at[0], f_recv.at[0])

    def select(i):
        marks, weights = [], 0.0
        for h in range(2):
            row_key = (
                lax.broadcasted_iota(jnp.int32, (S, zm.shape[3]), 0) + (z * S - h * CAP)
            ).astype(F32)
            table = zm[i, h]
            mark = 0.0
            for k in range(per_token):
                hit = table[k : k + 1, :] == row_key
                mark = mark + jnp.where(hit, 1.0, 0.0)
                weights = weights + jnp.where(hit, table[per_token + k : per_token + k + 1, :], 0.0)
            marks.append(mark)
        place = jnp.concatenate(marks, axis=1).astype(BF16)
        row_scale = jnp.sum(weights, axis=1, keepdims=True)
        picked_t = dot(place, zt[i].reshape(-1, Q)).astype(BF16)
        picked_g = (dot(place, zg[i].reshape(-1, Q)) * row_scale).astype(BF16)
        xs[i, :, :, 0:Q] = picked_t.reshape(J, PAIR, Q)
        xs[i, :, :, Q : 2 * Q] = picked_g.reshape(J, PAIR, Q)

    def z_stage(i):
        @pl.when(i >= 1)
        def _():
            for kind in (0, 2):
                z_copy(kind, 1, (i, 0), (i, 0)).wait_recv()

        @pl.when(i < R - 1)
        def _():
            for kind in (0, 2):
                z_copy(kind, 1, (i, 0), (i + 1, 0)).start()

        for kind in (0, 2):
            z_copy(kind, 0, (i, 1), (i, 1)).wait_recv()

        @pl.when(i < R - 1)
        def _():
            for kind in (0, 2):
                z_copy(kind, 0, (i, 1), (i + 1, 1)).start()

        @pl.when(i >= 1)
        def _():
            z_copy(1, 1, (i, 0), (i, 0)).wait_recv()

        @pl.when(i < R - 1)
        def _():
            z_copy(1, 1, (i, 0), (i + 1, 0)).start()

        @pl.when(i == R - 1)
        def _():
            z_copy(1, 1, (R - 1, 0), (R - 1, 1)).start()

        z_copy(1, 0, (i, 1), (i, 1)).wait_recv()

        @pl.when(i < R - 2)
        def _():
            z_copy(1, 0, (i, 1), (i + 1, 1)).start()

    def select_stage(i):
        select(i)
        exchange_start(0, i)

    def x_stage(i):
        exchange_wait(0, i)
        slot_t[y, i] = sx[i, :, :, 0:Q]
        gather(0, 0, i).start()
        gather(0, 1, i).start()

    def relay_stage(kind, i):
        buf = gather_buffer(kind)
        arrived(buf.at[pl.ds(0, 2), i], y_recv.at[kind, 0, i])
        gather(kind, 2, i).start()
        gather(kind, 3, i).start()

    def relay_wait(kind, i):
        arrived(gather_buffer(kind).at[yo, i], y_recv.at[kind, 1, i])

    def hidden_stage(i):
        relay_wait(0, i)
        rows = jnp.concatenate([slot_t[q, i].reshape(S, Q) for q in range(4)], axis=1)
        both = dot(wv[...].reshape(2 * F, 4 * Q), rows, NT)
        pre[i] = both
        g, u = both[0:F], both[F : 2 * F]
        hid[y, i] = (g * jax.nn.sigmoid(g) * u).astype(BF16)
        gather(1, 0, i).start()
        gather(1, 1, i).start()

    def down_stage(i):
        relay_wait(1, i)
        total = dot(hid[:, i].reshape(4 * F, S), dv[...], TN)
        eo[i] = total.astype(BF16).reshape(J, PAIR, Q)
        exchange_start(1, i)

    def return_stage(i):
        exchange_wait(1, i)
        row = lax.broadcasted_iota(jnp.int32, (S, S), 0)
        col = lax.broadcasted_iota(jnp.int32, (S, S), 1)
        h = lax.div(row, jnp.int32(C))
        j = lax.div(row - h * C, jnp.int32(CAP))
        source = j * PAIR + h * CAP + (row - h * C - j * CAP)
        swap = jnp.where(col == source, 1.0, 0.0).astype(BF16)
        rz[pl.ds(2 * i, 2)] = dot(swap, rx[i].reshape(S, Q)).astype(BF16).reshape(2, C, Q)

        @pl.when(i >= 1)
        def _():
            return_copy(0, i).start()

        @pl.when(i == 0)
        def _():
            return_own().start()

        return_copy(1, i).start()

    def sum_part(i):
        part = dot(dv[...], sx[i, :, :, Q : 2 * Q].reshape(S, Q), NT)
        hgp[i] = part.reshape(4, F, S)
        hgs[i, 0] = hgp[i, yo].astype(BF16)

    def sum_first(i):
        reduce(0, i).start()
        reduce(1, i).start()

    def sum_second(i):
        half = F // 2
        arrived(rs_half.at[i], s_recv.at[0, i])
        hgs[i, 1, 0:half] = (hgp[i, yp, 0:half] + rs_half[i, 0].astype(F32)).astype(BF16)
        hgs[i, 1, half:F] = hgp[i, yp, half:F].astype(BF16)
        reduce(2, i).start()
        hgs[i, 2, half:F] = (hgp[i, ym, half:F] + rs_half[i, 1].astype(F32)).astype(BF16)
        hgs[i, 2, 0:half] = hgp[i, ym, 0:half].astype(BF16)
        reduce(3, i).start()

    def sum_last(i):
        arrived(rs_full.at[i], s_recv.at[1, i])
        hidden_grad = hgp[i, y] + rs_full[i, 0].astype(F32) + rs_full[i, 1].astype(F32)
        g, u = pre[i, 0:F], pre[i, F : 2 * F]
        s = jax.nn.sigmoid(g)
        gate_grad = hidden_grad * u * s * (1.0 + g * (1.0 - s))
        up_grad = hidden_grad * (g * s)
        grads[i] = jnp.concatenate([gate_grad, up_grad], axis=0).astype(BF16)

    for kind in (0, 2, 1):
        z_copy(kind, 0, (0, 0), (0, 1)).start()

    delta = z - plane
    delta = jnp.where(delta < 0, delta + nz, delta)
    back = jnp.where(delta < R, delta * 2, (nz - 1 - delta) * 2 + 1)
    row_of = (back * C + member * CAP).astype(F32) + ranks
    packed = jnp.concatenate([row_of, scales], axis=0)
    tokens = packed.shape[1]
    packed = jnp.concatenate(
        [packed, jnp.zeros((tokens - 2 * per_token, tokens), F32)], axis=0
    ).T
    for r in range(R):
        lane = (lax.broadcasted_iota(jnp.int32, (tokens, 2 * C), 1) + r * 2 * C).astype(F32)
        weight = 0.0
        for k in range(per_token):
            hit = packed[:, k : k + 1] == lane
            weight = weight + jnp.where(hit, packed[:, per_token + k : per_token + k + 1], 0.0)
        for part in range(3):
            piece = weight.astype(BF16)
            place_v[part, :, r * 2 * C : (r + 1) * 2 * C] = piece
            weight = weight - piece.astype(F32)
    for load in loads[4:]:
        load.wait()

    stages = (
        (0, z_stage),
        (6, return_stage),
        (5, down_stage),
        (4, functools.partial(relay_stage, 1)),
        (3, hidden_stage),
        (2, functools.partial(relay_stage, 0)),
        (1, x_stage),
        (0, select_stage),
        (2, sum_part),
    )
    sums = ((10, sum_last), (9, sum_second), (8, sum_first))

    def step(i, carry):
        for lag, stage in stages:

            @pl.when((i >= lag) & (i < R + lag))
            def _(lag=lag, stage=stage):
                stage(i - lag)

        for lag, stage in sums:

            @pl.when((i >= lag) & (i < R // 2 + lag))
            def _(lag=lag, stage=stage):
                stage((i - lag) * 2)
                stage((i - lag) * 2 + 1)

        return carry

    lax.fori_loop(0, R + 6, step, 0)

    flat_g = sx[:, :, :, Q : 2 * Q].reshape(R * S, Q)
    for q in range(4):
        lhs = jnp.concatenate([hid[q, r] for r in range(R)], axis=1)
        down_out[q * F : (q + 1) * F] = dot(lhs, flat_g).astype(BF16)
    lhs = jnp.concatenate([grads[r] for r in range(R)], axis=1)
    for q in range(4):
        res = dot(lhs, slot_t[q].reshape(R * S, Q)).astype(BF16)
        gate_out[:, q * Q : (q + 1) * Q] = res[0:F]
        up_out[:, q * Q : (q + 1) * Q] = res[F : 2 * F]

    arrived(zt.at[:, 0], z_send.at[0, 0])
    arrived(zm.at[:, 0], z_send.at[0, 2])
    arrived(zg.at[pl.ds(0, R - 1), 0], z_send.at[0, 1])
    arrived(zt.at[pl.ds(0, R - 1), 0], z_send.at[1, 0])
    arrived(zm.at[pl.ds(0, R - 1), 0], z_send.at[1, 2])
    arrived(zg.at[:, 0], z_send.at[1, 1])
    arrived(xs.at[:, pl.ds(0, J - 1)], x_send.at[0])
    arrived(eo.at[:, pl.ds(0, J - 1)], x_send.at[1])
    arrived(slot_t.at[pl.ds(0, 3)], y_send.at[0])
    arrived(hid.at[pl.ds(0, 3)], y_send.at[1])
    arrived(hgs, s_send)
    near = 2 * (R - 2)
    total = 0.0
    for n, (low, count) in enumerate(((0, near), (near, 4))):
        arrived(fin.at[pl.ds(low, count)], f_recv.at[n])
        rows = fin[low : low + count].reshape(count * C, Q)
        for part in range(3):
            total = total + dot(place_v[part, :, low * C : (low + count) * C], rows)
    layer_out[...] = total.astype(BF16)
    arrived(rz.at[pl.ds(0, 2 * R - 1)], f_send)


def store_kernel(*refs):
    sems = refs[8]
    copies = [pltpu.make_async_copy(refs[n], refs[4 + n], sems.at[n]) for n in range(4)]
    for copy in copies:
        copy.start()
    for copy in copies:
        copy.wait()


def body(tokens, grad_out, expert_ids, gate_scale, gate_weight, up_weight, down_weight):
    nx = lax.axis_size("grp")
    nz = lax.axis_size("loc") // 2
    rows, Q = tokens.shape
    per_token = expert_ids.shape[1]
    F = gate_weight.shape[1]
    R, J = nz // 2, 2 * nx
    S, C = J * PAIR, J * CAP
    hbm = pl.BlockSpec(memory_space=pltpu.HBM)
    dma = pltpu.SemaphoreType.DMA
    outs = pl.pallas_call(
        functools.partial(layer_kernel, nx, nz),
        out_shape=(
            jax.ShapeDtypeStruct((rows, Q), BF16),
            jax.ShapeDtypeStruct((F, 4 * Q), BF16),
            jax.ShapeDtypeStruct((F, 4 * Q), BF16),
            jax.ShapeDtypeStruct((4 * F, Q), BF16),
        ),
        in_specs=[hbm] * 7,
        out_specs=(pl.BlockSpec(memory_space=pltpu.VMEM),) * 4,
        scratch_shapes=[
            pltpu.VMEM((per_token, rows), jnp.int32),
            pltpu.VMEM((per_token, rows), F32),
            pltpu.VMEM((2, F, 4 * Q), BF16),
            pltpu.VMEM((4 * F, Q), BF16),
            pltpu.VMEM((R, 2, rows, Q), BF16),
            pltpu.VMEM((R, 2, rows, Q), BF16),
            pltpu.VMEM((R, 2, 2 * per_token, rows), F32),
            pltpu.VMEM((R, J, PAIR, 2 * Q), BF16),
            pltpu.VMEM((R, J, PAIR, 2 * Q), BF16),
            pltpu.VMEM((4, R, J, PAIR, Q), BF16),
            pltpu.VMEM((R, 2 * F, S), F32),
            pltpu.VMEM((4, R, F, S), BF16),
            pltpu.VMEM((R, 4, F, S), F32),
            pltpu.VMEM((R, 3, F, S), BF16),
            pltpu.VMEM((R, 2, F // 2, S), BF16),
            pltpu.VMEM((R, 2, F, S), BF16),
            pltpu.VMEM((R, J, PAIR, Q), BF16),
            pltpu.VMEM((R, J, PAIR, Q), BF16),
            pltpu.VMEM((2 * R, C, Q), BF16),
            pltpu.VMEM((2 * R, C, Q), BF16),
            pltpu.VMEM((R, 2 * F, S), BF16),
            pltpu.VMEM((3, rows, R * S), BF16),
            dma((7,)),
            dma((2, 3)),
            dma((R, 2, 3)),
            dma((2,)),
            dma((2, R)),
            dma((2,)),
            dma((2, 2, R)),
            dma(()),
            dma((2, R)),
            dma(()),
            dma((2,)),
        ],
        compiler_params=pltpu.CompilerParams(
            collective_id=0, has_side_effects=True, vmem_limit_bytes=48 * 1024 * 1024
        ),
    )(
        *(
            pltpu.with_memory_space_constraint(a, pltpu.HBM)
            for a in (
                expert_ids.T,
                gate_scale.T,
                tokens,
                grad_out,
                gate_weight[0],
                up_weight[0],
                down_weight[0],
            )
        )
    )
    outs = pl.pallas_call(
        store_kernel,
        out_shape=tuple(jax.ShapeDtypeStruct(o.shape, o.dtype) for o in outs),
        in_specs=[pl.BlockSpec(memory_space=pltpu.VMEM)] * 4,
        out_specs=(hbm,) * 4,
        scratch_shapes=[dma((4,))],
        compiler_params=pltpu.CompilerParams(vmem_limit_bytes=8 * 1024 * 1024),
    )(*outs)
    return (outs[0], outs[1][None], outs[2][None], outs[3][None])


def solution(mesh):
    return jax.shard_map(
        body,
        mesh=mesh,
        in_specs=(
            P(("grp", "loc"), "dp"),
            P(("grp", "loc"), "dp"),
            P(("grp", "loc"), None),
            P(("grp", "loc"), None),
            P(("grp", "loc"), "dp", None),
            P(("grp", "loc"), "dp", None),
            P(("grp", "loc"), None, "dp"),
        ),
        out_specs=(
            P(("grp", "loc"), "dp"),
            P(("grp", "loc"), "dp", None),
            P(("grp", "loc"), "dp", None),
            P(("grp", "loc"), None, "dp"),
        ),
        check_vma=False,
    )
```
